32 devices in a mesh: dp: 2 (over y), fsdp: 16 (over z, x, core).
Axes of the slice: x: 2, y: 2, z: 4, core: 2. Of those that a mesh axis runs over, the one named last changes fastest.
Arguments:
- ids: int32 [2, 192], P('dp'), may hold values from 0 to 511
- embed: bfloat16 [512, 8192], P(None, 'fsdp'), may hold values from -32 to 32
- gain: bfloat16 [8192], P('fsdp'), may hold values from 0.099609375 to 1.8984375
- w_in: bfloat16 [3, 4096, 8192], P(None, 'fsdp'), may hold values from -0.0625 to 0.0625
- feat_filter: float32 [3, 256, 7], P(None, 'fsdp'), may hold values from -2.4 to 2.4
- inner_filter: float32 [256, 7], P('fsdp'), may hold values from -2.4 to 2.4
- w_out: bfloat16 [4096, 8192], P(None, 'fsdp'), may hold values from -0.09375 to 0.09375
- cotangent: bfloat16 [2, 192, 8192], P('dp', None, 'fsdp'), may hold values from -6 to 6
- right_prev: bfloat16 [8192, 256], P('fsdp'), may hold values from -6 to 6
Outputs:
- block_out: bfloat16 [2, 192, 8192], P('dp', None, 'fsdp')
- filter_grad: float32 [4, 256, 7], P(None, 'fsdp')
- basis: bfloat16 [4096, 256], P('fsdp')
- right_factor: float32 [8192, 256], P('fsdp')
The draws below stay inside these ranges and needn't reach their ends.
All inputs are finite; a program needn't handle non-finite values.
Results may differ from the reference program's by a relative error of at most 0.014.
The reference program's roundings to bfloat16 on the way count: a program that leaves them out, or rounds other values in their place, can miss the bound.
Values may be sent and summed in bfloat16 or wider, within the bound.
No kernel may reach another device: no remote copies, remote signals or barrier semaphores. Data moves between devices by JAX's collectives and lax.ppermute only.
A program may use at most 128 MiB of HBM per device.

```python
import jax
import jax.numpy as jnp
from jax import lax

D = 8192
VOCAB = 512
C = 4096
GROUP = 16
TAPS = 7
R = 256
SEQ_LEN = 192
SEQS = 2


def draw_embed(key, part):
    first_key, second_key = jax.random.split(jax.random.fold_in(key, 11), 2)
    column = jnp.arange(D, dtype=jnp.float32) / D
    jitter = jax.random.uniform(second_key, (1, D), jnp.float32, 0.5, 2.0)
    base = jnp.clip(jax.random.normal(first_key, (VOCAB, D), jnp.float32), -4.0, 4.0)
    rising = jnp.exp(column * jnp.log(3.0))
    return (base * rising[None, :] * jitter).astype(jnp.bfloat16)


def touch_ends(array, own_key, least, high):
    shape = array.shape
    spot = [jax.random.randint(jax.random.fold_in(own_key, axis), (), 0, shape[axis]) for axis in range(len(shape))]
    array = array.at[tuple(spot)].set(least)
    longest = shape.index(max(shape))
    spot[longest] = (spot[longest] + 1) % shape[longest]
    return array.at[tuple(spot)].set(high)


def block_scale(key, dims, cuts, smallest, top_value):
    loudness = 1.0
    for position, shards_of in cuts:
        steps = jax.random.uniform(jax.random.fold_in(jax.random.fold_in(key, 6), position), (shards_of,), jnp.float32, smallest / len(cuts), top_value / len(cuts))
        loudness = loudness * jnp.repeat(jnp.exp(steps), dims[position] // shards_of).reshape((-1,) + (1,) * (len(dims) - 1 - position))
    return loudness


def bell_draw(rng, extent, spread, reach, cuts=(), held_as=jnp.bfloat16):
    loudness = block_scale(rng, extent, cuts, -0.22, 0.18) if cuts else 1.0
    entries = jax.random.normal(rng, extent, jnp.float32) * spread * loudness
    return jnp.minimum(jnp.maximum(entries, -reach), reach).astype(held_as)


def setup_inputs(seed: int = 0) -> dict:
    keys = jax.random.split(jax.random.key(seed), 10)
    return {
        "ids": touch_ends(jax.random.randint(keys[0], (SEQS, SEQ_LEN), 0, VOCAB), jax.random.fold_in(keys[0], 1), 0, VOCAB - 1).astype(jnp.int32),
        "embed": draw_embed(jax.random.fold_in(keys[9], 71), 0),
        "gain": jnp.clip(1.0 + 0.18 * jax.random.normal(keys[2], (D,), jnp.float32), 0.099609375, 1.8984375).astype(jnp.bfloat16),
        "w_in": bell_draw(keys[3], (3, C, D), D ** -0.5, 0.0625, ((1, 16),)),
        "feat_filter": bell_draw(keys[4], (3, C // GROUP, TAPS), 0.4, 2.4, ((1, 16),), jnp.float32),
        "inner_filter": bell_draw(keys[5], (C // GROUP, TAPS), 0.4, 2.4, ((0, 16),), jnp.float32),
        "w_out": bell_draw(keys[6], (C, D), C ** -0.5, 0.09375, ((1, 16),)),
        "cotangent": bell_draw(keys[7], (SEQS, SEQ_LEN, D), 1.0, 6.0, ((0, 2), (2, 16))),
        "right_prev": bell_draw(keys[8], (D, R), 1.0, 6.0, ((0, 16),)),
    }


def shifted(signal, lag, tap_count):
    padded = jnp.pad(signal, ((tap_count - 1, 0), (0, 0)))
    first = tap_count - 1 - lag
    return padded[first:first + signal.shape[0]]

def causal(signal, tap_table):
    tap_count = tap_table.shape[0]
    result = jnp.zeros(signal.shape, jnp.float32)
    for lag in range(tap_count):
        result = result + tap_table[lag][None, :] * shifted(signal, lag, tap_count)
    return result

def anticausal(signal, tap_table):
    tap_count = tap_table.shape[0]
    padded = jnp.pad(signal, ((0, tap_count - 1), (0, 0)))
    result = jnp.zeros(signal.shape, jnp.float32)
    for lag in range(tap_count):
        result = result + tap_table[lag][None, :] * padded[lag:lag + signal.shape[0]]
    return result

def tap_sums(gradient, signal, tap_count):
    listing = []
    for lag in range(tap_count):
        listing.append(lax.optimization_barrier(jnp.sum(gradient * shifted(signal, lag, tap_count), axis=0)))
    stacked = jnp.stack(listing, axis=0)
    grouped = stacked.reshape(tap_count, stacked.shape[1] // GROUP, GROUP).sum(axis=2)
    return grouped.T

def expand(filters):
    return jnp.repeat(filters.T, GROUP, axis=1)

def sequence_pass(query, key_in, value, mixed_grad, feat_filter, inner_filter, norm_factor):
    tap_count = inner_filter.shape[1]
    query_conv = causal(query, expand(feat_filter[0]))
    key_conv = causal(key_in, expand(feat_filter[1]))
    value_conv = causal(value, expand(feat_filter[2]))
    gated = key_conv * value_conv
    window = causal(gated, expand(inner_filter))
    query_grad = mixed_grad * window
    window_grad = mixed_grad * query_conv
    gated_grad = anticausal(window_grad, expand(inner_filter))
    key_grad = gated_grad * value_conv
    value_grad = gated_grad * key_conv
    parts = jnp.stack([tap_sums(query_grad, query, tap_count), tap_sums(key_grad, key_in, tap_count), tap_sums(value_grad, value, tap_count), tap_sums(window_grad, gated, tap_count)], axis=0)
    return parts * norm_factor

def sequence_forward(query, key_in, value, feat_filter, inner_filter):
    query_conv = causal(query, expand(feat_filter[0]))
    key_conv = causal(key_in, expand(feat_filter[1]))
    value_conv = causal(value, expand(feat_filter[2]))
    window = causal(key_conv * value_conv, expand(inner_filter))
    return (query_conv * window).astype(jnp.bfloat16)

def reference(ids, embed, gain, w_in, feat_filter, inner_filter, w_out, cotangent, right_prev):
    x_half = embed[ids]
    x_full = x_half.astype(jnp.float32)
    square_mean = lax.optimization_barrier(jnp.mean(x_full * x_full, axis=-1, keepdims=True))
    normed = (x_full * lax.rsqrt(square_mean + 1e-05) * gain.astype(jnp.float32)).astype(jnp.bfloat16)
    flat = normed.reshape(SEQS * SEQ_LEN, D)
    projected = []
    for which in range(3):
        part = jnp.dot(flat.astype(jnp.float32), w_in[which].T.astype(jnp.float32), preferred_element_type=jnp.float32).astype(jnp.bfloat16)
        part = lax.optimization_barrier(part)
        projected.append(part.astype(jnp.float32).reshape(SEQS, SEQ_LEN, C))
    query, key_in, value = projected
    gated_out = jax.vmap(sequence_forward, in_axes=(0, 0, 0, None, None))(query, key_in, value, feat_filter, inner_filter)
    mixed = jnp.dot(gated_out.reshape(SEQS * SEQ_LEN, C).astype(jnp.float32), w_out.astype(jnp.float32), preferred_element_type=jnp.float32)
    block_out = (x_full.reshape(SEQS * SEQ_LEN, D) + mixed).astype(jnp.bfloat16).reshape(SEQS, SEQ_LEN, D)
    mixed_grad = jnp.dot(cotangent.reshape(SEQS * SEQ_LEN, D).astype(jnp.float32), w_out.T.astype(jnp.float32), preferred_element_type=jnp.float32)
    mixed_grad = mixed_grad.reshape(SEQS, SEQ_LEN, C)
    norm_factor = 1.0 / jnp.sqrt(jnp.float32(SEQS * SEQ_LEN))
    filter_parts = jax.vmap(sequence_pass, in_axes=(0, 0, 0, 0, None, None, None))(query, key_in, value, mixed_grad, feat_filter, inner_filter, norm_factor)
    filter_parts = lax.optimization_barrier(filter_parts.astype(jnp.bfloat16))
    filter_grad = lax.optimization_barrier(jnp.sum(filter_parts.astype(jnp.float32), axis=0))

    def add_sequence(running, which):
        term = jnp.dot(gated_out[which].T.astype(jnp.float32), cotangent[which].astype(jnp.float32), preferred_element_type=jnp.float32)
        term = lax.optimization_barrier(term.astype(jnp.bfloat16))
        return (running + term.astype(jnp.float32), None)
    grad_total, unused = lax.scan(add_sequence, jnp.zeros((C, D), jnp.float32), jnp.arange(SEQS))
    grad_half = grad_total.astype(jnp.bfloat16)
    panel_half = jnp.dot(grad_half.astype(jnp.float32), right_prev.astype(jnp.float32), preferred_element_type=jnp.float32).astype(jnp.bfloat16)
    gram_matrix = jnp.dot(panel_half.T.astype(jnp.float32), panel_half.astype(jnp.float32), preferred_element_type=jnp.float32)
    lower_factor = jnp.linalg.cholesky(gram_matrix)
    solved = jax.scipy.linalg.solve_triangular(lower_factor, panel_half.astype(jnp.float32).T, lower=True).T
    basis = (solved * jnp.sqrt(jnp.float32(C))).astype(jnp.bfloat16)
    right_raw = jnp.dot(grad_half.T.astype(jnp.float32), basis.astype(jnp.float32), preferred_element_type=jnp.float32)
    column_mean = lax.optimization_barrier(jnp.mean(right_raw * right_raw, axis=0, keepdims=True))
    right_factor = right_raw * lax.rsqrt(column_mean + 1e-06)
    return (block_out, filter_grad, basis, right_factor)
```

```python
import functools

import jax
import jax.numpy as jnp
from jax import lax
from jax.experimental import pallas as pl
from jax.experimental.pallas import tpu as pltpu
from jax.sharding import PartitionSpec as P

HIGH = lax.Precision.HIGHEST
F32 = jnp.float32
BF16 = jnp.bfloat16
EXTRA = 16


def exchange(value, axis, size, bits):
    return lax.ppermute(value, axis, [(i, i ^ bits) for i in range(size)])


def plane_gather(piece, size):
    if size != 16:
        whole = lax.all_gather(piece, "fsdp", axis=0)
        quarter = size // 4
        return [whole[i * quarter : (i + 1) * quarter] for i in range(4)]
    send = functools.partial(exchange, axis="fsdp", size=size)
    line = jnp.stack([piece] + [send(piece, bits=4 * step) for step in (1, 2, 3)])
    across = send(line, bits=2)
    return [line, across, send(line, bits=1), send(across, bits=1)]


def plane_order(size):
    if size != 16:
        return jnp.arange(size, dtype=jnp.int32)
    index = lax.axis_index("fsdp").astype(jnp.int32)
    slots = [(bit_x * 2 + bit_core) ^ (4 * step) for bit_core in (0, 1) for bit_x in (0, 1) for step in range(4)]
    return jnp.bitwise_xor(index, jnp.array(slots, jnp.int32))


def plane_sum(value, size):
    if size != 16:
        return lax.psum(value, "fsdp")
    send = functools.partial(exchange, axis="fsdp", size=size)
    value = value + send(value, bits=1)
    value = value + send(value, bits=2)
    return (value + send(value, bits=4)) + (send(value, bits=8) + send(value, bits=12))


def plane_scatter(parts, size):
    index = lax.axis_index("fsdp")
    if size != 16:
        return lax.psum_scatter(parts.astype(F32), "fsdp", scatter_dimension=0, tiled=True)[0]
    rows = parts.shape[1:]
    for bits, lead in ((1, 8), (2, 4), (8, 1), (4, 1)):
        if bits < 4:
            view = parts.reshape((lead, 2) + rows)
            axis, own = 1, (index // bits) % 2
        else:
            count = parts.shape[0]
            view = parts.reshape((2, count // 2) + rows)
            axis, own = 0, (index // bits) % 2
        sent = lax.dynamic_index_in_dim(view, 1 - own, axis, keepdims=False).astype(BF16)
        kept = lax.dynamic_index_in_dim(view, own, axis, keepdims=False).astype(F32)
        parts = kept + exchange(sent, "fsdp", size, bits).astype(F32)
    return parts[0]


def sequences(value, count):
    if count != 2:
        gathered = lax.all_gather(value, "dp", axis=0)
        return [gathered[i] for i in range(count)]
    other = exchange(value, "dp", count, 1)
    first = lax.axis_index("dp") == 0
    return [jnp.where(first, value, other), jnp.where(first, other, value)]


def spread(table, width):
    group = width // table.shape[-2]
    return jnp.repeat(jnp.swapaxes(table, -1, -2), group, axis=-1)


def pad_front(pad, signal):
    length = signal.shape[0]
    pad[pl.ds(0, 8), :] = jnp.zeros((8, signal.shape[1]), F32)
    pad[pl.ds(8, length), :] = signal


def lagged(pad, lag, length):
    return pad[pl.ds(8 - lag, length), :]


def mix_kernel(order, *refs, length, cut, width):
    early, late, weights = refs[0:4], refs[4:8], refs[8:12]
    feat, inner = refs[12:14]
    y_out, qkv_out, saved = refs[14:17]
    acc, factor, pad = refs[17:20]
    step = pl.program_id(0)
    taps = inner.shape[0]

    @pl.when(step == 0)
    def _():
        top = jnp.zeros((cut, 1), F32)
        low = jnp.zeros((length - cut, 1), F32)
        for slot in range(early[0].shape[0]):
            for side in range(4):
                a = early[side][slot].astype(F32)
                b = late[side][slot, : length - cut, :].astype(F32)
                top = top + jnp.sum(a * a, axis=1, keepdims=True)
                low = low + jnp.sum(b * b, axis=1, keepdims=True)
        squares = jnp.concatenate([top, low], axis=0)
        factor[...] = jnp.broadcast_to(lax.rsqrt(squares / width + 1e-05), factor.shape)
        acc[...] = jnp.zeros_like(acc)

    scale = factor[:, 0:1]
    for side in range(4):
        gain = late[side][step, pl.ds(length - cut, EXTRA), :][0:1].astype(F32)
        a = early[side][step].astype(F32)
        b = late[side][step, pl.ds(0, length - cut), :].astype(F32)
        normed = (jnp.concatenate([a, b], axis=0) * scale * gain).astype(BF16)
        for which in range(3):
            acc[which] += lax.dot_general(
                normed, weights[side][which], (((1,), (1,)), ((), ())), preferred_element_type=F32
            )

    @pl.when(step == pl.num_programs(0) - 1)
    def _():
        convs = []
        for which in range(3):
            half = acc[which].astype(BF16)
            qkv_out[which] = half
            pad_front(pad, half.astype(F32))
            total = jnp.zeros((length, acc.shape[2]), F32)
            for lag in range(taps):
                total = total + feat[which, lag : lag + 1, :] * lagged(pad, lag, length)
            convs.append(total)
            saved[which] = total
        gated = convs[1] * convs[2]
        saved[3] = gated
        pad_front(pad, gated)
        window = jnp.zeros(gated.shape, F32)
        for lag in range(taps):
            window = window + inner[lag : lag + 1, :] * lagged(pad, lag, length)
        saved[4] = window
        y_out[...] = (convs[0] * window).astype(BF16)


def mix(order, early, late, w_in, feat, inner):
    slots, cut, width = early[0].shape
    length = cut + late[0].shape[1] - EXTRA
    local = w_in.shape[1]
    taps = inner.shape[0]
    full = lambda shape: pl.BlockSpec(shape, lambda i, o: (0,) * len(shape))
    weight = lambda side: pl.BlockSpec((3, local, width), lambda i, o: (0, 0, o[side * slots + i]))
    return pl.pallas_call(
        functools.partial(mix_kernel, length=length, cut=cut, width=w_in.shape[2]),
        out_shape=(
            jax.ShapeDtypeStruct((length, local), BF16),
            jax.ShapeDtypeStruct((3, length, local), BF16),
            jax.ShapeDtypeStruct((5, length, local), F32),
        ),
        grid_spec=pltpu.PrefetchScalarGridSpec(
            num_scalar_prefetch=1,
            grid=(slots,),
            in_specs=[full(e.shape) for e in early]
            + [full(e.shape) for e in late]
            + [weight(side) for side in range(4)]
            + [full(feat.shape), full(inner.shape)],
            out_specs=(full((length, local)), full((3, length, local)), full((5, length, local))),
            scratch_shapes=[
                pltpu.VMEM((3, length, local), F32),
                pltpu.VMEM((length, 128), F32),
                pltpu.VMEM((length + 16, local), F32),
            ],
        ),
        compiler_params=pltpu.CompilerParams(
            dimension_semantics=("arbitrary",), vmem_limit_bytes=48 * 2**20
        ),
        name="mix",
    )(order, *early, *late, w_in, w_in, w_in, w_in, feat, inner)


def taps_kernel(grad, qkv, saved, inner, pool, out, pad, stack):
    length = grad.shape[0]
    taps = inner.shape[0]
    given = grad[...]
    query_conv, key_conv, value_conv = saved[0], saved[1], saved[2]
    query_grad = given * saved[4]
    window_grad = given * query_conv
    pad[pl.ds(0, length), :] = window_grad
    pad[pl.ds(length, 8), :] = jnp.zeros((8, given.shape[1]), F32)
    gated_grad = jnp.zeros(given.shape, F32)
    for lag in range(taps):
        gated_grad = gated_grad + inner[lag : lag + 1, :] * pad[pl.ds(lag, length), :]
    pairs = (
        (query_grad, qkv[0].astype(F32)),
        (gated_grad * value_conv, qkv[1].astype(F32)),
        (gated_grad * key_conv, qkv[2].astype(F32)),
        (window_grad, saved[3]),
    )
    stack[...] = jnp.zeros_like(stack)
    for row, (gradient, signal) in enumerate(pairs):
        pad_front(pad, signal)
        for lag in range(taps):
            stack[8 * row + lag : 8 * row + lag + 1, :] = jnp.sum(
                gradient * lagged(pad, lag, length), axis=0, keepdims=True
            )
    out[...] = lax.dot_general(
        stack[...], pool[...], (((1,), (0,)), ((), ())), precision=HIGH, preferred_element_type=F32
    )


def filter_taps(grad, qkv, saved, inner, groups):
    length, local = grad.shape
    member = jnp.arange(local)[:, None] // (local // groups) == jnp.arange(groups)[None, :]
    out = pl.pallas_call(
        taps_kernel,
        out_shape=jax.ShapeDtypeStruct((32, groups), F32),
        scratch_shapes=[pltpu.VMEM((length + 16, local), F32), pltpu.VMEM((32, local), F32)],
        name="filter_taps",
    )(grad, qkv, saved, inner, member.astype(F32))
    return jnp.swapaxes(out.reshape(4, 8, groups), 1, 2)[:, :, : inner.shape[0]]


def out_kernel(order, *refs, length):
    sides, weights, x, out, acc = refs[0:4], refs[4:8], refs[8], refs[9], refs[10]
    step = pl.program_id(0)

    @pl.when(step == 0)
    def _():
        acc[...] = jnp.zeros_like(acc)

    total = acc[...]
    for side in range(4):
        total = total + jnp.dot(
            sides[side][0, :length, :], weights[side][...], preferred_element_type=F32
        )
    acc[...] = total

    @pl.when(step == pl.num_programs(0) - 1)
    def _():
        out[...] = (x[...].astype(F32) + total).astype(BF16)


def project(order, sides, w_out, x):
    length, width = x.shape
    slots, rows, local = sides[0].shape
    full = lambda shape: pl.BlockSpec(shape, lambda i, o: (0,) * len(shape))
    weight = lambda side: pl.BlockSpec((local, width), lambda i, o: (o[side * slots + i], 0))
    return pl.pallas_call(
        functools.partial(out_kernel, length=length),
        out_shape=jax.ShapeDtypeStruct((length, width), BF16),
        grid_spec=pltpu.PrefetchScalarGridSpec(
            num_scalar_prefetch=1,
            grid=(slots,),
            in_specs=[pl.BlockSpec((1, rows, local), lambda i, o: (i, 0, 0)) for _ in range(4)]
            + [weight(side) for side in range(4)]
            + [full((length, width))],
            out_specs=full((length, width)),
            scratch_shapes=[pltpu.VMEM((length, width), F32)],
        ),
        compiler_params=pltpu.CompilerParams(dimension_semantics=("arbitrary",)),
        name="project",
    )(order, *sides, w_out, w_out, w_out, w_out, x)


def eliminate(block):
    size = block.shape[0]
    row = lax.broadcasted_iota(jnp.int32, (size, size), 0)
    lane = lax.broadcasted_iota(jnp.int32, (size, size), 1)
    both = jnp.concatenate([block, (row == lane).astype(F32)], axis=1)
    tiles = [both[8 * i : 8 * i + 8, :] for i in range(size // 8)]
    inside = lax.broadcasted_iota(jnp.int32, (8, 1), 0)
    for j in range(size):
        at, off = divmod(j, 8)
        pivot = tiles[at][off : off + 1, :]
        inverse = 1.0 / pivot[:, j : j + 1]
        for i in range(at, size // 8):
            if i == at and off == 7:
                continue
            share = tiles[i][:, j : j + 1] * inverse
            if i == at:
                share = jnp.where(inside > off, share, 0.0)
            tiles[i] = tiles[i] - share * pivot
    both = jnp.concatenate(tiles, axis=0)
    diagonal = jnp.sum(jnp.where(row == lane, both[:, :size], 0.0), axis=1, keepdims=True)
    return both[:, size:] * lax.rsqrt(diagonal)


def dot_high(a, b, contract):
    return lax.dot_general(a, b, (contract, ((), ())), precision=HIGH, preferred_element_type=F32)


def factor_kernel(gram, out):
    half = gram.shape[0] // 2
    first = eliminate(gram[:half, :half])
    below = dot_high(gram[half:, :half], first, ((1,), (1,)))
    rest = gram[half:, half:] - dot_high(below, below, ((1,), (1,)))
    second = eliminate(rest)
    corner = -dot_high(second, dot_high(below, first, ((1,), (0,))), ((1,), (0,)))
    out[:half, :half] = first
    out[:half, half:] = jnp.zeros((half, half), F32)
    out[half:, :half] = corner
    out[half:, half:] = second


def inverse_factor(gram):
    return pl.pallas_call(
        factor_kernel,
        out_shape=jax.ShapeDtypeStruct(gram.shape, F32),
        name="inverse_factor",
    )(gram)


def per_device(ids, embed, gain, w_in, feat_filter, inner_filter, w_out, cotangent, right_prev):
    size = lax.axis_size("fsdp")
    count = lax.axis_size("dp")
    tokens = ids[0]
    length = tokens.shape[0]
    vocab, width = embed.shape
    local = w_in.shape[1]
    rank = right_prev.shape[1]
    cut = length // 2
    order = plane_order(size)

    onehot = (tokens[:, None] == jnp.arange(vocab, dtype=jnp.int32)[None, :]).astype(BF16)
    x_cols = jnp.dot(onehot, embed, preferred_element_type=F32).astype(BF16)
    tail = jnp.broadcast_to(gain[None, :], (EXTRA, width))
    early = plane_gather(x_cols[:cut], size)
    late = plane_gather(jnp.concatenate([x_cols[cut:], tail], axis=0), size)

    cot_cols = cotangent[0]
    parts = jnp.einsum(
        "scd,ld->slc", w_out.reshape(size, local, width), cot_cols, preferred_element_type=F32
    ).astype(BF16)
    side = lax.dot_general(right_prev, cot_cols, (((0,), (1,)), ((), ())), preferred_element_type=F32)
    share = rank // size
    if length <= local:
        packed = jnp.pad(side, ((0, 0), (0, local - length))).reshape(size, share, local)
        summed = plane_scatter(jnp.concatenate([parts, packed.astype(BF16)], axis=1), size)
        y_grad = summed[:length]
        side_own = summed[length:]
        high = side_own.astype(BF16)
        low = (side_own - high.astype(F32)).astype(BF16)
        rider = jnp.concatenate([high, low], axis=0)
    else:
        y_grad = plane_scatter(parts, size)
        rider = jnp.zeros((0, local), BF16)

    feat = spread(feat_filter, local)
    inner = spread(inner_filter, local)
    y, qkv, saved = mix(order, early, late, w_in, feat, inner)

    sent = jnp.concatenate([y, rider], axis=0)
    y_seqs = sequences(sent, count)
    gathered = [plane_gather(piece, size) for piece in y_seqs]
    rows = [jnp.concatenate(sides, axis=0) for sides in gathered]
    mine = lax.axis_index("dp")
    own_sides = [
        lax.dynamic_index_in_dim(jnp.stack([g[i] for g in gathered]), mine, 0, keepdims=False)
        for i in range(4)
    ]
    block_out = project(order, own_sides, w_out, x_cols)[None]

    stacked = jnp.stack([r[:, :length] for r in rows])
    flat = stacked.transpose(0, 2, 1, 3).reshape(count * length, size * local)
    kernel_m = lax.dot_general(flat, flat, (((1,), (1,)), ((), ())), preferred_element_type=F32)
    if length <= local:
        slots = jnp.argsort(order)
        pieces = []
        for r in rows:
            part = r[:, length : length + share].astype(F32) + r[:, length + share :].astype(F32)
            pieces.append(part[slots].reshape(rank, local)[:, :length].T)
        weights = jnp.concatenate(pieces, axis=0)
    else:
        weights = jnp.concatenate(sequences(lax.psum(side, "fsdp").T, count), axis=0)
    product = jnp.dot(kernel_m, weights, precision=HIGH)
    gram = dot_high(weights, product, ((0,), (0,)))
    inverse = inverse_factor(gram) * jnp.sqrt(F32(size * local))
    y_both = jnp.concatenate([p[:length] for p in y_seqs], axis=0).astype(F32)
    panel = dot_high(y_both, weights, ((0,), (0,)))
    basis = dot_high(panel, inverse, ((1,), (1,))).astype(BF16)
    turned = dot_high(product, inverse, ((1,), (1,)))
    cot_both = jnp.concatenate(sequences(cot_cols, count), axis=0).astype(F32)
    right_raw = dot_high(cot_both, turned, ((0,), (0,)))
    column_sums = plane_sum(jnp.sum(right_raw * right_raw, axis=0, keepdims=True), size)
    right_factor = right_raw * lax.rsqrt(column_sums / (size * width) + 1e-06)

    norm_factor = 1.0 / jnp.sqrt(F32(count * length))
    terms = filter_taps(y_grad, qkv, saved, inner, feat_filter.shape[1]) * norm_factor
    halves = sequences(terms.astype(BF16), count)
    filter_grad = sum(h.astype(F32) for h in halves)
    return (block_out, filter_grad, basis, right_factor)


def solution(mesh):
    placed = (
        P("dp", None),
        P(None, "fsdp"),
        P("fsdp"),
        P(None, "fsdp", None),
        P(None, "fsdp", None),
        P("fsdp", None),
        P(None, "fsdp"),
        P("dp", None, "fsdp"),
        P("fsdp", None),
    )
    return jax.shard_map(
        per_device,
        mesh=mesh,
        in_specs=placed,
        out_specs=(P("dp", None, "fsdp"), P(None, "fsdp", None), P("fsdp", None), P("fsdp", None)),
        check_vma=False,
    )
```

```python
import functools
import math

import jax
import jax.numpy as jnp
from jax import lax
from jax.experimental import pallas as pl
from jax.experimental.pallas import tpu as pltpu
from jax.sharding import PartitionSpec as P

HIGH = lax.Precision.HIGHEST
F32 = jnp.float32
BF16 = jnp.bfloat16
EXTRA = 16


def exchange(value, axis, size, bits):
    return lax.ppermute(value, axis, [(i, i ^ bits) for i in range(size)])


def plane_gather(piece, size):
    if size != 16:
        whole = lax.all_gather(piece, "fsdp", axis=0)
        quarter = size // 4
        return [whole[i * quarter : (i + 1) * quarter] for i in range(4)]
    send = functools.partial(exchange, axis="fsdp", size=size)
    line = jnp.stack([piece] + [send(piece, bits=4 * step) for step in (1, 2, 3)])
    across = send(line, bits=2)
    return [line, across, send(line, bits=1), send(across, bits=1)]


def plane_order(size):
    if size != 16:
        return jnp.arange(size, dtype=jnp.int32)
    index = lax.axis_index("fsdp").astype(jnp.int32)
    slots = [(bit_x * 2 + bit_core) ^ (4 * step) for bit_core in (0, 1) for bit_x in (0, 1) for step in range(4)]
    return jnp.bitwise_xor(index, jnp.array(slots, jnp.int32))


def plane_sum(value, size):
    if size != 16:
        return lax.psum(value, "fsdp")
    send = functools.partial(exchange, axis="fsdp", size=size)
    value = value + send(value, bits=1)
    value = value + send(value, bits=2)
    value = value + send(value, bits=4)
    return value + send(value, bits=8)


def plane_scatter(parts, size):
    index = lax.axis_index("fsdp")
    if size != 16:
        return lax.psum_scatter(parts.astype(F32), "fsdp", scatter_dimension=0, tiled=True)[0]
    rows = parts.shape[1:]
    for bits, lead in ((1, 8), (2, 4), (8, 1), (4, 1)):
        if bits < 4:
            view = parts.reshape((lead, 2) + rows)
            axis, own = 1, (index // bits) % 2
        else:
            count = parts.shape[0]
            view = parts.reshape((2, count // 2) + rows)
            axis, own = 0, (index // bits) % 2
        sent = lax.dynamic_index_in_dim(view, 1 - own, axis, keepdims=False).astype(BF16)
        kept = lax.dynamic_index_in_dim(view, own, axis, keepdims=False).astype(F32)
        parts = kept + exchange(sent, "fsdp", size, bits).astype(F32)
    return parts[0]


def sequences(value, count):
    if count != 2:
        gathered = lax.all_gather(value, "dp", axis=0)
        return [gathered[i] for i in range(count)]
    other = exchange(value, "dp", count, 1)
    first = lax.axis_index("dp") == 0
    return [jnp.where(first, value, other), jnp.where(first, other, value)]


def spread(table, width):
    group = width // table.shape[-2]
    return jnp.repeat(jnp.swapaxes(table, -1, -2), group, axis=-1)


def pad_front(pad, signal):
    length = signal.shape[0]
    pad[pl.ds(0, 8), :] = jnp.zeros((8, signal.shape[1]), F32)
    pad[pl.ds(8, length), :] = signal


def lagged(pad, lag, length):
    return pad[pl.ds(8 - lag, length), :]


def mix_kernel(order, *refs, length, cut, width):
    early, late, weights = refs[0:4], refs[4:8], refs[8:12]
    feat, inner = refs[12:14]
    y_out, qkv_out, saved = refs[14:17]
    acc, factor, pad = refs[17:20]
    step = pl.program_id(0)
    taps = inner.shape[0]

    @pl.when(step == 0)
    def _():
        top = jnp.zeros((cut, 1), F32)
        low = jnp.zeros((length - cut, 1), F32)
        for slot in range(early[0].shape[0]):
            for side in range(4):
                a = early[side][slot].astype(F32)
                b = late[side][slot, : length - cut, :].astype(F32)
                top = top + jnp.sum(a * a, axis=1, keepdims=True)
                low = low + jnp.sum(b * b, axis=1, keepdims=True)
        squares = jnp.concatenate([top, low], axis=0)
        factor[...] = jnp.broadcast_to(lax.rsqrt(squares / width + 1e-05), factor.shape)
        acc[...] = jnp.zeros_like(acc)

    scale = factor[:, 0:1]
    for side in range(4):
        gain = late[side][step, pl.ds(length - cut, EXTRA), :][0:1].astype(F32)
        a = early[side][step].astype(F32)
        b = late[side][step, pl.ds(0, length - cut), :].astype(F32)
        normed = (jnp.concatenate([a, b], axis=0) * scale * gain).astype(BF16)
        for which in range(3):
            acc[which] += lax.dot_general(
                normed, weights[side][which], (((1,), (1,)), ((), ())), preferred_element_type=F32
            )

    @pl.when(step == pl.num_programs(0) - 1)
    def _():
        convs = []
        for which in range(3):
            half = acc[which].astype(BF16)
            qkv_out[which] = half
            pad_front(pad, half.astype(F32))
            total = jnp.zeros((length, acc.shape[2]), F32)
            for lag in range(taps):
                total = total + feat[which, lag : lag + 1, :] * lagged(pad, lag, length)
            convs.append(total)
            saved[which] = total
        gated = convs[1] * convs[2]
        saved[3] = gated
        pad_front(pad, gated)
        window = jnp.zeros(gated.shape, F32)
        for lag in range(taps):
            window = window + inner[lag : lag + 1, :] * lagged(pad, lag, length)
        saved[4] = window
        y_out[...] = (convs[0] * window).astype(BF16)


def mix(order, early, late, w_in, feat, inner):
    slots, cut, width = early[0].shape
    length = cut + late[0].shape[1] - EXTRA
    local = w_in.shape[1]
    taps = inner.shape[0]
    full = lambda shape: pl.BlockSpec(shape, lambda i, o: (0,) * len(shape))
    weight = lambda side: pl.BlockSpec((3, local, width), lambda i, o: (0, 0, o[side * slots + i]))
    return pl.pallas_call(
        functools.partial(mix_kernel, length=length, cut=cut, width=w_in.shape[2]),
        out_shape=(
            jax.ShapeDtypeStruct((length, local), BF16),
            jax.ShapeDtypeStruct((3, length, local), BF16),
            jax.ShapeDtypeStruct((5, length, local), F32),
        ),
        grid_spec=pltpu.PrefetchScalarGridSpec(
            num_scalar_prefetch=1,
            grid=(slots,),
            in_specs=[full(e.shape) for e in early]
            + [full(e.shape) for e in late]
            + [weight(side) for side in range(4)]
            + [full(feat.shape), full(inner.shape)],
            out_specs=(full((length, local)), full((3, length, local)), full((5, length, local))),
            scratch_shapes=[
                pltpu.VMEM((3, length, local), F32),
                pltpu.VMEM((length, 128), F32),
                pltpu.VMEM((length + 16, local), F32),
            ],
        ),
        compiler_params=pltpu.CompilerParams(
            dimension_semantics=("arbitrary",), vmem_limit_bytes=48 * 2**20
        ),
        name="mix",
    )(order, *early, *late, w_in, w_in, w_in, w_in, feat, inner)


def taps_kernel(grad, qkv, saved, inner, pool, out, pad, stack):
    length = grad.shape[0]
    taps = inner.shape[0]
    given = grad[...]
    query_conv, key_conv, value_conv = saved[0], saved[1], saved[2]
    query_grad = given * saved[4]
    window_grad = given * query_conv
    pad[pl.ds(0, length), :] = window_grad
    pad[pl.ds(length, 8), :] = jnp.zeros((8, given.shape[1]), F32)
    gated_grad = jnp.zeros(given.shape, F32)
    for lag in range(taps):
        gated_grad = gated_grad + inner[lag : lag + 1, :] * pad[pl.ds(lag, length), :]
    pairs = (
        (query_grad, qkv[0].astype(F32)),
        (gated_grad * value_conv, qkv[1].astype(F32)),
        (gated_grad * key_conv, qkv[2].astype(F32)),
        (window_grad, saved[3]),
    )
    stack[...] = jnp.zeros_like(stack)
    for row, (gradient, signal) in enumerate(pairs):
        pad_front(pad, signal)
        for lag in range(taps):
            stack[8 * row + lag : 8 * row + lag + 1, :] = jnp.sum(
                gradient * lagged(pad, lag, length), axis=0, keepdims=True
            )
    out[...] = lax.dot_general(
        stack[...], pool[...], (((1,), (0,)), ((), ())), precision=HIGH, preferred_element_type=F32
    )


def filter_taps(grad, qkv, saved, inner, groups):
    length, local = grad.shape
    member = jnp.arange(local)[:, None] // (local // groups) == jnp.arange(groups)[None, :]
    out = pl.pallas_call(
        taps_kernel,
        out_shape=jax.ShapeDtypeStruct((32, groups), F32),
        scratch_shapes=[pltpu.VMEM((length + 16, local), F32), pltpu.VMEM((32, local), F32)],
        name="filter_taps",
    )(grad, qkv, saved, inner, member.astype(F32))
    return jnp.swapaxes(out.reshape(4, 8, groups), 1, 2)[:, :, : inner.shape[0]]


def out_kernel(order, *refs, length):
    sides, weights, x, out, acc = refs[0:4], refs[4:8], refs[8], refs[9], refs[10]
    step = pl.program_id(0)

    @pl.when(step == 0)
    def _():
        acc[...] = jnp.zeros_like(acc)

    total = acc[...]
    for side in range(4):
        total = total + jnp.dot(
            sides[side][0, :length, :], weights[side][...], preferred_element_type=F32
        )
    acc[...] = total

    @pl.when(step == pl.num_programs(0) - 1)
    def _():
        out[...] = (x[...].astype(F32) + total).astype(BF16)


def project(order, sides, w_out, x):
    length, width = x.shape
    slots, rows, local = sides[0].shape
    full = lambda shape: pl.BlockSpec(shape, lambda i, o: (0,) * len(shape))
    weight = lambda side: pl.BlockSpec((local, width), lambda i, o: (o[side * slots + i], 0))
    return pl.pallas_call(
        functools.partial(out_kernel, length=length),
        out_shape=jax.ShapeDtypeStruct((length, width), BF16),
        grid_spec=pltpu.PrefetchScalarGridSpec(
            num_scalar_prefetch=1,
            grid=(slots,),
            in_specs=[pl.BlockSpec((1, rows, local), lambda i, o: (i, 0, 0)) for _ in range(4)]
            + [weight(side) for side in range(4)]
            + [full((length, width))],
            out_specs=full((length, width)),
            scratch_shapes=[pltpu.VMEM((length, width), F32)],
        ),
        compiler_params=pltpu.CompilerParams(dimension_semantics=("arbitrary",)),
        name="project",
    )(order, *sides, w_out, w_out, w_out, w_out, x)


def out_whole_kernel(order, *refs, length, local):
    count = len(RELATIVE)
    pieces, weights, x, out = refs[:count], refs[count], refs[count + 1], refs[count + 2]
    here, sems = refs[count + 3 :]
    for copy in copies_in(weights, here, sems):
        copy.wait()
    total = x[:length, :].astype(F32)
    for slot, piece in enumerate(pieces):
        place = pl.ds(pl.multiple_of(order[slot] * local, local), local)
        total = total + jnp.dot(piece[:length, :], here[place, :], preferred_element_type=F32)
    out[...] = total.astype(BF16)


def project_whole(order, pieces, w_out, x):
    width = x.shape[1]
    length = x.shape[0] - EXTRA
    local = pieces[0].shape[1]
    whole = pl.BlockSpec(memory_space=pltpu.VMEM)
    return pl.pallas_call(
        functools.partial(out_whole_kernel, length=length, local=local),
        out_shape=jax.ShapeDtypeStruct((length, width), BF16),
        in_specs=[pl.BlockSpec(memory_space=pltpu.SMEM)]
        + [whole] * len(pieces)
        + [pl.BlockSpec(memory_space=pltpu.HBM), whole],
        out_specs=whole,
        scratch_shapes=[pltpu.VMEM(w_out.shape, w_out.dtype), pltpu.SemaphoreType.DMA((8,))],
        compiler_params=pltpu.CompilerParams(vmem_limit_bytes=16 * 2**20),
        cost_estimate=FREE,
        name="project",
    )(order, *pieces, w_out, x)


def eliminate(block):
    size = block.shape[0]
    row = lax.broadcasted_iota(jnp.int32, (size, size), 0)
    lane = lax.broadcasted_iota(jnp.int32, (size, size), 1)
    unit = (row == lane).astype(F32)
    left = [block[8 * i : 8 * i + 8, :] for i in range(size // 8)]
    right = [unit[8 * i : 8 * i + 8, :] for i in range(size // 8)]
    inside = lax.broadcasted_iota(jnp.int32, (8, size), 0)
    wide = lambda tile, j: jnp.broadcast_to(tile[:, j : j + 1], (8, size))
    for at in range(size // 8):
        a, v = left[at], right[at]
        cols = [wide(a, 8 * at + k) for k in range(8)]
        inverses = []
        for k in range(8):
            inverse = 1.0 / cols[k][k : k + 1, :]
            inverses.append(inverse)
            share = jnp.where(inside > k, cols[k] * inverse, 0.0)
            for l in range(k + 1, 8):
                cols[l] = cols[l] - share * cols[l][k : k + 1, :]
            a = a - share * a[k : k + 1, :]
            v = v - share * v[k : k + 1, :]
        left[at], right[at] = a, v
        for i in range(at + 1, size // 8):
            mine = [wide(left[i], 8 * at + k) for k in range(8)]
            p, q = left[i], right[i]
            for k in range(8):
                share = mine[k] * inverses[k]
                for l in range(k + 1, 8):
                    mine[l] = mine[l] - share * cols[l][k : k + 1, :]
                p = p - share * a[k : k + 1, :]
                q = q - share * v[k : k + 1, :]
            left[i], right[i] = p, q
    upper = jnp.concatenate(left, axis=0)
    diagonal = jnp.sum(jnp.where(row == lane, upper, 0.0), axis=1, keepdims=True)
    return jnp.concatenate(right, axis=0) * lax.rsqrt(diagonal)


def dot_high(a, b, contract):
    return lax.dot_general(a, b, (contract, ((), ())), precision=HIGH, preferred_element_type=F32)


def factor_kernel(gram, out):
    half = gram.shape[0] // 2
    first = eliminate(gram[:half, :half])
    below = dot_high(gram[half:, :half], first, ((1,), (1,)))
    rest = gram[half:, half:] - dot_high(below, below, ((1,), (1,)))
    second = eliminate(rest)
    corner = -dot_high(second, dot_high(below, first, ((1,), (0,))), ((1,), (0,)))
    out[:half, :half] = first
    out[:half, half:] = jnp.zeros((half, half), F32)
    out[half:, :half] = corner
    out[half:, half:] = second


def inverse_factor(gram):
    return pl.pallas_call(
        factor_kernel,
        out_shape=jax.ShapeDtypeStruct(gram.shape, F32),
        name="inverse_factor",
    )(gram)


def general_device(ids, embed, gain, w_in, feat_filter, inner_filter, w_out, cotangent, right_prev):
    size = lax.axis_size("fsdp")
    count = lax.axis_size("dp")
    tokens = ids[0]
    length = tokens.shape[0]
    vocab, width = embed.shape
    local = w_in.shape[1]
    rank = right_prev.shape[1]
    cut = length // 2
    order = plane_order(size)

    onehot = (tokens[:, None] == jnp.arange(vocab, dtype=jnp.int32)[None, :]).astype(BF16)
    x_cols = jnp.dot(onehot, embed, preferred_element_type=F32).astype(BF16)
    tail = jnp.broadcast_to(gain[None, :], (EXTRA, width))
    early = plane_gather(x_cols[:cut], size)
    late = plane_gather(jnp.concatenate([x_cols[cut:], tail], axis=0), size)

    cot_cols = cotangent[0]
    parts = jnp.einsum(
        "scd,ld->slc", w_out.reshape(size, local, width), cot_cols, preferred_element_type=F32
    ).astype(BF16)
    side = lax.dot_general(right_prev, cot_cols, (((0,), (1,)), ((), ())), preferred_element_type=F32)
    share = rank // size
    if length <= local:
        packed = jnp.pad(side, ((0, 0), (0, local - length))).reshape(size, share, local)
        summed = plane_scatter(jnp.concatenate([parts, packed.astype(BF16)], axis=1), size)
        y_grad = summed[:length]
        side_own = summed[length:]
        high = side_own.astype(BF16)
        low = (side_own - high.astype(F32)).astype(BF16)
        rider = jnp.concatenate([high, low], axis=0)
    else:
        y_grad = plane_scatter(parts, size)
        rider = jnp.zeros((0, local), BF16)

    feat = spread(feat_filter, local)
    inner = spread(inner_filter, local)
    y, qkv, saved = mix(order, early, late, w_in, feat, inner)

    sent = jnp.concatenate([y, rider], axis=0)
    y_seqs = sequences(sent, count)
    gathered = [plane_gather(piece, size) for piece in y_seqs]
    rows = [jnp.concatenate(sides, axis=0) for sides in gathered]
    mine = lax.axis_index("dp")
    own_sides = [
        lax.dynamic_index_in_dim(jnp.stack([g[i] for g in gathered]), mine, 0, keepdims=False)
        for i in range(4)
    ]
    block_out = project(order, own_sides, w_out, x_cols)[None]

    stacked = jnp.stack([r[:, :length] for r in rows])
    flat = stacked.transpose(0, 2, 1, 3).reshape(count * length, size * local)
    kernel_m = lax.dot_general(flat, flat, (((1,), (1,)), ((), ())), preferred_element_type=F32)
    if length <= local:
        slots = jnp.argsort(order)
        pieces = []
        for r in rows:
            part = r[:, length : length + share].astype(F32) + r[:, length + share :].astype(F32)
            pieces.append(part[slots].reshape(rank, local)[:, :length].T)
        weights = jnp.concatenate(pieces, axis=0)
    else:
        weights = jnp.concatenate(sequences(lax.psum(side, "fsdp").T, count), axis=0)
    product = jnp.dot(kernel_m, weights, precision=HIGH)
    gram = dot_high(weights, product, ((0,), (0,)))
    inverse = inverse_factor(gram) * jnp.sqrt(F32(size * local))
    y_both = jnp.concatenate([p[:length] for p in y_seqs], axis=0).astype(F32)
    panel = dot_high(y_both, weights, ((0,), (0,)))
    basis = dot_high(panel, inverse, ((1,), (1,))).astype(BF16)
    turned = dot_high(product, inverse, ((1,), (1,)))
    cot_both = jnp.concatenate(sequences(cot_cols, count), axis=0).astype(F32)
    right_raw = dot_high(cot_both, turned, ((0,), (0,)))
    column_sums = plane_sum(jnp.sum(right_raw * right_raw, axis=0, keepdims=True), size)
    right_factor = right_raw * lax.rsqrt(column_sums / (size * width) + 1e-06)

    norm_factor = 1.0 / jnp.sqrt(F32(count * length))
    terms = filter_taps(y_grad, qkv, saved, inner, feat_filter.shape[1]) * norm_factor
    halves = sequences(terms.astype(BF16), count)
    filter_grad = sum(h.astype(F32) for h in halves)
    return (block_out, filter_grad, basis, right_factor)


def finish_kernel(flag, *refs):
    count = len(RELATIVE)
    pieces = refs[:count]
    side_own, side_other, cot_own, cot_other = refs[count : count + 4]
    basis, right_raw, sums = refs[count + 4 : count + 7]
    rows, cots, sides, inverse = refs[count + 7 :]
    mine = flag[0]
    other = 1 - mine
    length = cots.shape[1]
    local = pieces[0].shape[1]
    for at, piece in enumerate(pieces):
        lanes = slice(at * local, (at + 1) * local)
        rows[mine, :, lanes] = piece[:length, :]
        rows[other, :, lanes] = piece[length:, :]
    sides[mine] = side_own[...]
    sides[other] = side_other[...]
    cots[mine] = cot_own[...]
    cots[other] = cot_other[...]
    turned = [sides[0], sides[1]]
    first, second = rows[0], rows[1]
    transposed = ((1,), (1,))
    plain = ((1,), (0,))
    soft = lambda a, b, contract: lax.dot_general(a, b, (contract, ((), ())), preferred_element_type=F32)
    corner = soft(first, first, transposed)
    across = soft(first, second, transposed)
    across_t = soft(second, first, transposed)
    end = soft(second, second, transposed)
    upper = dot_high(corner, turned[0], plain) + dot_high(across, turned[1], plain)
    under = dot_high(across_t, turned[0], plain) + dot_high(end, turned[1], plain)
    rowwise = ((0,), (0,))
    gram = dot_high(turned[0], upper, rowwise) + dot_high(turned[1], under, rowwise)
    factor_kernel(gram, inverse)
    scaled = inverse[...] * math.sqrt(local * count)
    panel = jnp.zeros((local, gram.shape[0]), F32)
    for i in (0, 1):
        own = jnp.where(mine == i, pieces[0][:length, :], pieces[0][length:, :])
        top = turned[i].astype(BF16)
        rest = (turned[i] - top.astype(F32)).astype(BF16)
        panel = panel + soft(own, top, rowwise) + soft(own, rest, rowwise)
    basis[...] = dot_high(panel, scaled, transposed).astype(BF16)
    raw = jnp.zeros(right_raw.shape, F32)
    for i, product in enumerate((upper, under)):
        turn = dot_high(product, scaled, transposed)
        top = turn.astype(BF16)
        rest = (turn - top.astype(F32)).astype(BF16)
        raw = raw + soft(cots[i], top, ((0,), (0,))) + soft(cots[i], rest, ((0,), (0,)))
    right_raw[...] = raw
    sums[...] = jnp.sum(raw * raw, axis=0, keepdims=True)


def finish(flag, pieces, side_own, side_other, cot_own, cot_other):
    local = pieces[0].shape[1]
    length, width = cot_own.shape
    rank = side_own.shape[1]
    count = len(pieces)
    whole = pl.BlockSpec(memory_space=pltpu.VMEM)
    return pl.pallas_call(
        finish_kernel,
        out_shape=(
            jax.ShapeDtypeStruct((local, rank), BF16),
            jax.ShapeDtypeStruct((width, rank), F32),
            jax.ShapeDtypeStruct((1, rank), F32),
        ),
        in_specs=[pl.BlockSpec(memory_space=pltpu.SMEM)] + [whole] * (count + 4),
        out_specs=(whole, whole, whole),
        scratch_shapes=[
            pltpu.VMEM((2, length, count * local), BF16),
            pltpu.VMEM((2, length, width), BF16),
            pltpu.VMEM((2, length, rank), F32),
            pltpu.VMEM((rank, rank), F32),
        ],
        compiler_params=pltpu.CompilerParams(vmem_limit_bytes=20 * 2**20),
        cost_estimate=pl.CostEstimate(flops=2**33, transcendentals=0, bytes_accessed=2**22),
        name="finish",
    )(flag, *pieces, side_own, side_other, cot_own, cot_other)


FREE = pl.CostEstimate(flops=1, transcendentals=0, bytes_accessed=1)


def copies_in(source, target, sems):
    count = sems.shape[0]
    rows = source.shape[0] // count
    copies = []
    for i in range(count):
        part = pl.ds(i * rows, rows)
        copies.append(pltpu.make_async_copy(source.at[part], target.at[part], sems.at[i]))
        copies[-1].start()
    return copies


def parts_kernel(order, weights, cot, send, keep, here, sems, *, local):
    half = send.shape[0]
    for copy in copies_in(weights, here, sems):
        copy.wait()
    for slot in range(2 * half):
        out, at = (send, slot) if slot < half else (keep, slot - half)
        rows = here[pl.ds(pl.multiple_of(order[slot] * local, local), local), :]
        out[at] = lax.dot_general(
            cot[...], rows, (((1,), (1,)), ((), ())), preferred_element_type=F32
        ).astype(BF16)


def grad_parts(order, w_out, cot, size):
    length = cot.shape[0]
    local, half = w_out.shape[0] // size, size // 2
    shape = jax.ShapeDtypeStruct((half, length, local), BF16)
    whole = pl.BlockSpec(memory_space=pltpu.VMEM)
    return pl.pallas_call(
        functools.partial(parts_kernel, local=local),
        out_shape=(shape, shape),
        in_specs=[pl.BlockSpec(memory_space=pltpu.SMEM), pl.BlockSpec(memory_space=pltpu.HBM), whole],
        out_specs=(whole, whole),
        scratch_shapes=[pltpu.VMEM(w_out.shape, w_out.dtype), pltpu.SemaphoreType.DMA((8,))],
        compiler_params=pltpu.CompilerParams(vmem_limit_bytes=16 * 2**20),
        cost_estimate=FREE,
        name="grad_parts",
    )(order, w_out, cot)


RELATIVE = (0, 2, 4, 6, 8, 10, 12, 14, 1, 3, 5, 7, 9, 11, 13, 15)


def mix_whole_kernel(order, *refs, length):
    count = len(RELATIVE)
    pieces, weights = refs[:count], refs[count]
    feat, inner = refs[count + 1 : count + 3]
    y_out, qkv_out, saved = refs[count + 3 : count + 6]
    normed, pad, here, sems = refs[count + 6 :]
    copies = [copies_in(weights.at[i], here.at[i], sems.at[i]) for i in range(3)]
    taps = inner.shape[0]
    step = pieces[0].shape[1]
    squares = jnp.zeros((length, step), F32)
    for piece in pieces:
        a = piece[:length, :].astype(F32)
        squares = squares + a * a
    scale = lax.rsqrt(jnp.sum(squares, axis=1, keepdims=True) / (step * count) + 1e-05)
    for slot, piece in enumerate(pieces):
        place = pl.ds(pl.multiple_of(order[slot] * step, step), step)
        gain = piece[length:, :][0:1].astype(F32)
        normed[:, place] = (piece[:length, :].astype(F32) * scale * gain).astype(BF16)
    convs = []
    for which in range(3):
        for copy in copies[which]:
            copy.wait()
        half = lax.dot_general(
            normed[...], here[which], (((1,), (1,)), ((), ())), preferred_element_type=F32
        ).astype(BF16)
        qkv_out[which] = half
        pad_front(pad, half.astype(F32))
        result = jnp.zeros(half.shape, F32)
        for lag in range(taps):
            result = result + feat[which, lag : lag + 1, :] * lagged(pad, lag, length)
        convs.append(result)
        saved[which] = result
    gated = convs[1] * convs[2]
    saved[3] = gated
    pad_front(pad, gated)
    window = jnp.zeros(gated.shape, F32)
    for lag in range(taps):
        window = window + inner[lag : lag + 1, :] * lagged(pad, lag, length)
    saved[4] = window
    y_out[...] = (convs[0] * window).astype(BF16)


def mix_whole(order, pieces, w_in, feat, inner):
    rows, step = pieces[0].shape
    length = rows - EXTRA
    local, width = w_in.shape[1:]
    whole = pl.BlockSpec(memory_space=pltpu.VMEM)
    return pl.pallas_call(
        functools.partial(mix_whole_kernel, length=length),
        out_shape=(
            jax.ShapeDtypeStruct((length, local), BF16),
            jax.ShapeDtypeStruct((3, length, local), BF16),
            jax.ShapeDtypeStruct((5, length, local), F32),
        ),
        in_specs=[pl.BlockSpec(memory_space=pltpu.SMEM)]
        + [whole] * len(pieces)
        + [pl.BlockSpec(memory_space=pltpu.HBM), whole, whole],
        out_specs=(whole, whole, whole),
        scratch_shapes=[
            pltpu.VMEM((length, width), BF16),
            pltpu.VMEM((length + 16, local), F32),
            pltpu.VMEM(w_in.shape, w_in.dtype),
            pltpu.SemaphoreType.DMA((3, 4)),
        ],
        compiler_params=pltpu.CompilerParams(vmem_limit_bytes=24 * 2**20),
        cost_estimate=pl.CostEstimate(
            flops=6 * length * local * width, transcendentals=0, bytes_accessed=6 * local * width
        ),
        name="mix",
    )(order, *pieces, w_in, feat, inner)


def after(value, *events):
    return lax.optimization_barrier((value,) + events)[0]


def terms_kernel(summed, qkv, saved, inner, pool, out, pad, stack, sums, *, scale):
    taps_kernel(summed, qkv, saved, inner, pool, sums, pad, stack)
    out[...] = (sums[...] * scale).astype(BF16)


def filter_terms(summed, qkv, saved, inner, groups, scale):
    length, local = qkv.shape[1:]
    member = jnp.arange(local)[:, None] // (local // groups) == jnp.arange(groups)[None, :]
    return pl.pallas_call(
        functools.partial(terms_kernel, scale=scale),
        out_shape=jax.ShapeDtypeStruct((32, groups), BF16),
        scratch_shapes=[
            pltpu.VMEM((length + 16, local), F32),
            pltpu.VMEM((32, local), F32),
            pltpu.VMEM((32, groups), F32),
        ],
        cost_estimate=FREE,
        name="filter_terms",
    )(summed, qkv, saved, inner, member.astype(F32))


def hop_all(piece, size):
    send = functools.partial(exchange, axis="fsdp", size=size)
    have = {0: piece}
    for z in (4, 8, 12):
        have[z] = send(piece, bits=z)
    for z in (0, 4, 8, 12):
        have[z + 2] = send(have[z], bits=2)
    for near in (0, 4, 2, 6, 8, 10, 12, 14):
        have[near + 1] = send(have[near], bits=1)
    return have


def both_ways(value, bits, size):
    half = value.astype(BF16)
    return half.astype(F32) + exchange(half, "fsdp", size, bits).astype(F32)


def tuned_device(ids, embed, gain, w_in, feat_filter, inner_filter, w_out, cotangent, right_prev):
    size = lax.axis_size("fsdp")
    count = lax.axis_size("dp")
    tokens = ids[0]
    length = tokens.shape[0]
    vocab, width = embed.shape
    local = w_in.shape[1]
    rank = right_prev.shape[1]
    index = lax.axis_index("fsdp").astype(jnp.int32)
    order = jnp.bitwise_xor(index, jnp.array(RELATIVE, jnp.int32))
    flag = lax.axis_index("dp").astype(jnp.int32)[None]
    send = functools.partial(exchange, axis="fsdp", size=size)
    feat = spread(feat_filter, local)
    inner = spread(inner_filter, local)

    onehot = (tokens[:, None] == jnp.arange(vocab, dtype=jnp.int32)[None, :]).astype(BF16)
    x_cols = jnp.dot(onehot, embed, preferred_element_type=F32).astype(BF16)
    x_sent = jnp.concatenate([x_cols, jnp.broadcast_to(gain[None, :], (EXTRA, width))], axis=0)
    have = hop_all(x_sent, size)
    w_in = pltpu.with_memory_space_constraint(w_in, pltpu.HBM)
    w_out = pltpu.with_memory_space_constraint(w_out, pltpu.HBM)

    cot_cols = cotangent[0]
    turns = [c + x + f + n for c in (1, 0) for x in (2, 0) for f in (8, 0) for n in (4, 0)]
    targets = jnp.bitwise_xor(index, jnp.array(turns, jnp.int32))
    away, keep = grad_parts(targets, w_out, cot_cols, size)
    keep = keep.astype(F32) + send(away, bits=1).astype(F32)
    away, keep = keep[:4].astype(BF16), keep[4:]
    keep = keep + send(away, bits=2).astype(F32)
    away, keep = keep[:2].astype(BF16), keep[2:]
    side = jnp.dot(cot_cols, right_prev, preferred_element_type=F32)
    side = both_ways(side, 1, size)
    ready = after(order, side, away, keep)
    y, qkv, saved = mix_whole(ready, [have[r] for r in RELATIVE], w_in, feat, inner)

    keep = keep + send(away, bits=8).astype(F32)
    y_grad = (keep[1:] + send(keep[:1].astype(BF16), bits=4).astype(F32))[0]
    for bits in (2, 4, 8):
        side = both_ways(side, bits, size)
    side_other = exchange(side, "dp", count, 1)

    y_other = exchange(y, "dp", count, 1)
    got = hop_all(jnp.concatenate([y, y_other], axis=0), size)
    cot_other = exchange(after(cot_cols, got[4]), "dp", count, 1)
    groups = feat_filter.shape[1]
    scale = 1.0 / math.sqrt(count * length)
    terms = filter_terms(after(y_grad, got[12]), qkv, saved, inner, groups, scale)
    terms_other = exchange(terms, "dp", count, 1)
    filter_grad = terms.astype(F32) + terms_other.astype(F32)
    filter_grad = jnp.swapaxes(filter_grad.reshape(4, 8, groups), 1, 2)[:, :, : inner.shape[0]]
    got[15] = send(after(got[14], terms), bits=1)
    pieces = [got[r] for r in RELATIVE]
    basis, right_raw, sums = finish(flag, pieces, side, side_other, cot_cols, cot_other)
    column_sums = plane_sum(sums, size)
    block_out = project_whole(order, pieces, w_out, x_sent)[None]
    right_factor = right_raw * lax.rsqrt(column_sums / (size * width) + 1e-06)
    return (block_out, filter_grad, basis, right_factor)


def per_device(ids, embed, gain, w_in, feat_filter, inner_filter, w_out, cotangent, right_prev):
    sizes = (lax.axis_size("dp"), lax.axis_size("fsdp"))
    shapes = (ids.shape[1], w_in.shape[1], right_prev.shape[1])
    body = tuned_device if sizes == (2, 16) and shapes == (192, 256, 256) else general_device
    return body(ids, embed, gain, w_in, feat_filter, inner_filter, w_out, cotangent, right_prev)


def solution(mesh):
    placed = (
        P("dp", None),
        P(None, "fsdp"),
        P("fsdp"),
        P(None, "fsdp", None),
        P(None, "fsdp", None),
        P("fsdp", None),
        P(None, "fsdp"),
        P("dp", None, "fsdp"),
        P("fsdp", None),
    )
    return jax.shard_map(
        per_device,
        mesh=mesh,
        in_specs=placed,
        out_specs=(P("dp", None, "fsdp"), P(None, "fsdp", None), P("fsdp", None), P("fsdp", None)),
        check_vma=False,
    )
```

```python
import functools
import math

import jax
import jax.numpy as jnp
from jax import lax
from jax.experimental import pallas as pl
from jax.experimental.pallas import tpu as pltpu
from jax.sharding import PartitionSpec as P

HIGH = lax.Precision.HIGHEST
F32 = jnp.float32
BF16 = jnp.bfloat16
EXTRA = 16


def exchange(value, axis, size, bits):
    return lax.ppermute(value, axis, [(i, i ^ bits) for i in range(size)])


def plane_gather(piece, size):
    if size != 16:
        whole = lax.all_gather(piece, "fsdp", axis=0)
        quarter = size // 4
        return [whole[i * quarter : (i + 1) * quarter] for i in range(4)]
    send = functools.partial(exchange, axis="fsdp", size=size)
    line = jnp.stack([piece] + [send(piece, bits=4 * step) for step in (1, 2, 3)])
    across = send(line, bits=2)
    return [line, across, send(line, bits=1), send(across, bits=1)]


def plane_order(size):
    if size != 16:
        return jnp.arange(size, dtype=jnp.int32)
    index = lax.axis_index("fsdp").astype(jnp.int32)
    slots = [(bit_x * 2 + bit_core) ^ (4 * step) for bit_core in (0, 1) for bit_x in (0, 1) for step in range(4)]
    return jnp.bitwise_xor(index, jnp.array(slots, jnp.int32))


def plane_sum(value, size):
    if size != 16:
        return lax.psum(value, "fsdp")
    send = functools.partial(exchange, axis="fsdp", size=size)
    value = value + send(value, bits=1)
    value = value + send(value, bits=2)
    value = value + send(value, bits=4)
    return value + send(value, bits=8)


def plane_scatter(parts, size):
    index = lax.axis_index("fsdp")
    if size != 16:
        return lax.psum_scatter(parts.astype(F32), "fsdp", scatter_dimension=0, tiled=True)[0]
    rows = parts.shape[1:]
    for bits, lead in ((1, 8), (2, 4), (8, 1), (4, 1)):
        if bits < 4:
            view = parts.reshape((lead, 2) + rows)
            axis, own = 1, (index // bits) % 2
        else:
            count = parts.shape[0]
            view = parts.reshape((2, count // 2) + rows)
            axis, own = 0, (index // bits) % 2
        sent = lax.dynamic_index_in_dim(view, 1 - own, axis, keepdims=False).astype(BF16)
        kept = lax.dynamic_index_in_dim(view, own, axis, keepdims=False).astype(F32)
        parts = kept + exchange(sent, "fsdp", size, bits).astype(F32)
    return parts[0]


def sequences(value, count):
    if count != 2:
        gathered = lax.all_gather(value, "dp", axis=0)
        return [gathered[i] for i in range(count)]
    other = exchange(value, "dp", count, 1)
    first = lax.axis_index("dp") == 0
    return [jnp.where(first, value, other), jnp.where(first, other, value)]


def spread(table, width):
    group = width // table.shape[-2]
    return jnp.repeat(jnp.swapaxes(table, -1, -2), group, axis=-1)


def pad_front(pad, signal):
    length = signal.shape[0]
    pad[pl.ds(0, 8), :] = jnp.zeros((8, signal.shape[1]), F32)
    pad[pl.ds(8, length), :] = signal


def lagged(pad, lag, length):
    return pad[pl.ds(8 - lag, length), :]


def mix_kernel(order, *refs, length, cut, width):
    early, late, weights = refs[0:4], refs[4:8], refs[8:12]
    feat, inner = refs[12:14]
    y_out, qkv_out, saved = refs[14:17]
    acc, factor, pad = refs[17:20]
    step = pl.program_id(0)
    taps = inner.shape[0]

    @pl.when(step == 0)
    def _():
        top = jnp.zeros((cut, 1), F32)
        low = jnp.zeros((length - cut, 1), F32)
        for slot in range(early[0].shape[0]):
            for side in range(4):
                a = early[side][slot].astype(F32)
                b = late[side][slot, : length - cut, :].astype(F32)
                top = top + jnp.sum(a * a, axis=1, keepdims=True)
                low = low + jnp.sum(b * b, axis=1, keepdims=True)
        squares = jnp.concatenate([top, low], axis=0)
        factor[...] = jnp.broadcast_to(lax.rsqrt(squares / width + 1e-05), factor.shape)
        acc[...] = jnp.zeros_like(acc)

    scale = factor[:, 0:1]
    for side in range(4):
        gain = late[side][step, pl.ds(length - cut, EXTRA), :][0:1].astype(F32)
        a = early[side][step].astype(F32)
        b = late[side][step, pl.ds(0, length - cut), :].astype(F32)
        normed = (jnp.concatenate([a, b], axis=0) * scale * gain).astype(BF16)
        for which in range(3):
            acc[which] += lax.dot_general(
                normed, weights[side][which], (((1,), (1,)), ((), ())), preferred_element_type=F32
            )

    @pl.when(step == pl.num_programs(0) - 1)
    def _():
        convs = []
        for which in range(3):
            half = acc[which].astype(BF16)
            qkv_out[which] = half
            pad_front(pad, half.astype(F32))
            total = jnp.zeros((length, acc.shape[2]), F32)
            for lag in range(taps):
                total = total + feat[which, lag : lag + 1, :] * lagged(pad, lag, length)
            convs.append(total)
            saved[which] = total
        gated = convs[1] * convs[2]
        saved[3] = gated
        pad_front(pad, gated)
        window = jnp.zeros(gated.shape, F32)
        for lag in range(taps):
            window = window + inner[lag : lag + 1, :] * lagged(pad, lag, length)
        saved[4] = window
        y_out[...] = (convs[0] * window).astype(BF16)


def mix(order, early, late, w_in, feat, inner):
    slots, cut, width = early[0].shape
    length = cut + late[0].shape[1] - EXTRA
    local = w_in.shape[1]
    taps = inner.shape[0]
    full = lambda shape: pl.BlockSpec(shape, lambda i, o: (0,) * len(shape))
    weight = lambda side: pl.BlockSpec((3, local, width), lambda i, o: (0, 0, o[side * slots + i]))
    return pl.pallas_call(
        functools.partial(mix_kernel, length=length, cut=cut, width=w_in.shape[2]),
        out_shape=(
            jax.ShapeDtypeStruct((length, local), BF16),
            jax.ShapeDtypeStruct((3, length, local), BF16),
            jax.ShapeDtypeStruct((5, length, local), F32),
        ),
        grid_spec=pltpu.PrefetchScalarGridSpec(
            num_scalar_prefetch=1,
            grid=(slots,),
            in_specs=[full(e.shape) for e in early]
            + [full(e.shape) for e in late]
            + [weight(side) for side in range(4)]
            + [full(feat.shape), full(inner.shape)],
            out_specs=(full((length, local)), full((3, length, local)), full((5, length, local))),
            scratch_shapes=[
                pltpu.VMEM((3, length, local), F32),
                pltpu.VMEM((length, 128), F32),
                pltpu.VMEM((length + 16, local), F32),
            ],
        ),
        compiler_params=pltpu.CompilerParams(
            dimension_semantics=("arbitrary",), vmem_limit_bytes=48 * 2**20
        ),
        name="mix",
    )(order, *early, *late, w_in, w_in, w_in, w_in, feat, inner)


def taps_kernel(grad, qkv, saved, inner, pool, out, pad, stack):
    length = grad.shape[0]
    taps = inner.shape[0]
    given = grad[...]
    query_conv, key_conv, value_conv = saved[0], saved[1], saved[2]
    query_grad = given * saved[4]
    window_grad = given * query_conv
    pad[pl.ds(0, length), :] = window_grad
    pad[pl.ds(length, 8), :] = jnp.zeros((8, given.shape[1]), F32)
    gated_grad = jnp.zeros(given.shape, F32)
    for lag in range(taps):
        gated_grad = gated_grad + inner[lag : lag + 1, :] * pad[pl.ds(lag, length), :]
    pairs = (
        (query_grad, qkv[0].astype(F32)),
        (gated_grad * value_conv, qkv[1].astype(F32)),
        (gated_grad * key_conv, qkv[2].astype(F32)),
        (window_grad, saved[3]),
    )
    stack[...] = jnp.zeros_like(stack)
    for row, (gradient, signal) in enumerate(pairs):
        pad_front(pad, signal)
        for lag in range(taps):
            stack[8 * row + lag : 8 * row + lag + 1, :] = jnp.sum(
                gradient * lagged(pad, lag, length), axis=0, keepdims=True
            )
    out[...] = lax.dot_general(
        stack[...], pool[...], (((1,), (0,)), ((), ())), precision=HIGH, preferred_element_type=F32
    )


def filter_taps(grad, qkv, saved, inner, groups):
    length, local = grad.shape
    member = jnp.arange(local)[:, None] // (local // groups) == jnp.arange(groups)[None, :]
    out = pl.pallas_call(
        taps_kernel,
        out_shape=jax.ShapeDtypeStruct((32, groups), F32),
        scratch_shapes=[pltpu.VMEM((length + 16, local), F32), pltpu.VMEM((32, local), F32)],
        name="filter_taps",
    )(grad, qkv, saved, inner, member.astype(F32))
    return jnp.swapaxes(out.reshape(4, 8, groups), 1, 2)[:, :, : inner.shape[0]]


def out_kernel(order, *refs, length):
    sides, weights, x, out, acc = refs[0:4], refs[4:8], refs[8], refs[9], refs[10]
    step = pl.program_id(0)

    @pl.when(step == 0)
    def _():
        acc[...] = jnp.zeros_like(acc)

    total = acc[...]
    for side in range(4):
        total = total + jnp.dot(
            sides[side][0, :length, :], weights[side][...], preferred_element_type=F32
        )
    acc[...] = total

    @pl.when(step == pl.num_programs(0) - 1)
    def _():
        out[...] = (x[...].astype(F32) + total).astype(BF16)


def project(order, sides, w_out, x):
    length, width = x.shape
    slots, rows, local = sides[0].shape
    full = lambda shape: pl.BlockSpec(shape, lambda i, o: (0,) * len(shape))
    weight = lambda side: pl.BlockSpec((local, width), lambda i, o: (o[side * slots + i], 0))
    return pl.pallas_call(
        functools.partial(out_kernel, length=length),
        out_shape=jax.ShapeDtypeStruct((length, width), BF16),
        grid_spec=pltpu.PrefetchScalarGridSpec(
            num_scalar_prefetch=1,
            grid=(slots,),
            in_specs=[pl.BlockSpec((1, rows, local), lambda i, o: (i, 0, 0)) for _ in range(4)]
            + [weight(side) for side in range(4)]
            + [full((length, width))],
            out_specs=full((length, width)),
            scratch_shapes=[pltpu.VMEM((length, width), F32)],
        ),
        compiler_params=pltpu.CompilerParams(dimension_semantics=("arbitrary",)),
        name="project",
    )(order, *sides, w_out, w_out, w_out, w_out, x)


def eliminate(block):
    size = block.shape[0]
    row = lax.broadcasted_iota(jnp.int32, (size, size), 0)
    lane = lax.broadcasted_iota(jnp.int32, (size, size), 1)
    unit = (row == lane).astype(F32)
    left = [block[8 * i : 8 * i + 8, :] for i in range(size // 8)]
    right = [unit[8 * i : 8 * i + 8, :] for i in range(size // 8)]
    inside = lax.broadcasted_iota(jnp.int32, (8, size), 0)
    wide = lambda tile, j: jnp.broadcast_to(tile[:, j : j + 1], (8, size))
    for at in range(size // 8):
        a, v = left[at], right[at]
        cols = [wide(a, 8 * at + k) for k in range(8)]
        inverses = []
        for k in range(8):
            inverse = 1.0 / cols[k][k : k + 1, :]
            inverses.append(inverse)
            share = jnp.where(inside > k, cols[k] * inverse, 0.0)
            for l in range(k + 1, 8):
                cols[l] = cols[l] - share * cols[l][k : k + 1, :]
            a = a - share * a[k : k + 1, :]
            v = v - share * v[k : k + 1, :]
        left[at], right[at] = a, v
        for i in range(at + 1, size // 8):
            mine = [wide(left[i], 8 * at + k) for k in range(8)]
            p, q = left[i], right[i]
            for k in range(8):
                share = mine[k] * inverses[k]
                for l in range(k + 1, 8):
                    mine[l] = mine[l] - share * cols[l][k : k + 1, :]
                p = p - share * a[k : k + 1, :]
                q = q - share * v[k : k + 1, :]
            left[i], right[i] = p, q
    upper = jnp.concatenate(left, axis=0)
    diagonal = jnp.sum(jnp.where(row == lane, upper, 0.0), axis=1, keepdims=True)
    return jnp.concatenate(right, axis=0) * lax.rsqrt(diagonal)


def dot_high(a, b, contract):
    return lax.dot_general(a, b, (contract, ((), ())), precision=HIGH, preferred_element_type=F32)


def factor_kernel(gram, out):
    half = gram.shape[0] // 2
    first = eliminate(gram[:half, :half])
    below = dot_high(gram[half:, :half], first, ((1,), (1,)))
    rest = gram[half:, half:] - dot_high(below, below, ((1,), (1,)))
    second = eliminate(rest)
    corner = -dot_high(second, dot_high(below, first, ((1,), (0,))), ((1,), (0,)))
    out[:half, :half] = first
    out[:half, half:] = jnp.zeros((half, half), F32)
    out[half:, :half] = corner
    out[half:, half:] = second


def inverse_factor(gram):
    return pl.pallas_call(
        factor_kernel,
        out_shape=jax.ShapeDtypeStruct(gram.shape, F32),
        name="inverse_factor",
    )(gram)


def general_device(ids, embed, gain, w_in, feat_filter, inner_filter, w_out, cotangent, right_prev):
    size = lax.axis_size("fsdp")
    count = lax.axis_size("dp")
    tokens = ids[0]
    length = tokens.shape[0]
    vocab, width = embed.shape
    local = w_in.shape[1]
    rank = right_prev.shape[1]
    cut = length // 2
    order = plane_order(size)

    onehot = (tokens[:, None] == jnp.arange(vocab, dtype=jnp.int32)[None, :]).astype(BF16)
    x_cols = jnp.dot(onehot, embed, preferred_element_type=F32).astype(BF16)
    tail = jnp.broadcast_to(gain[None, :], (EXTRA, width))
    early = plane_gather(x_cols[:cut], size)
    late = plane_gather(jnp.concatenate([x_cols[cut:], tail], axis=0), size)

    cot_cols = cotangent[0]
    parts = jnp.einsum(
        "scd,ld->slc", w_out.reshape(size, local, width), cot_cols, preferred_element_type=F32
    ).astype(BF16)
    side = lax.dot_general(right_prev, cot_cols, (((0,), (1,)), ((), ())), preferred_element_type=F32)
    share = rank // size
    if length <= local:
        packed = jnp.pad(side, ((0, 0), (0, local - length))).reshape(size, share, local)
        summed = plane_scatter(jnp.concatenate([parts, packed.astype(BF16)], axis=1), size)
        y_grad = summed[:length]
        side_own = summed[length:]
        high = side_own.astype(BF16)
        low = (side_own - high.astype(F32)).astype(BF16)
        rider = jnp.concatenate([high, low], axis=0)
    else:
        y_grad = plane_scatter(parts, size)
        rider = jnp.zeros((0, local), BF16)

    feat = spread(feat_filter, local)
    inner = spread(inner_filter, local)
    y, qkv, saved = mix(order, early, late, w_in, feat, inner)

    sent = jnp.concatenate([y, rider], axis=0)
    y_seqs = sequences(sent, count)
    gathered = [plane_gather(piece, size) for piece in y_seqs]
    rows = [jnp.concatenate(sides, axis=0) for sides in gathered]
    mine = lax.axis_index("dp")
    own_sides = [
        lax.dynamic_index_in_dim(jnp.stack([g[i] for g in gathered]), mine, 0, keepdims=False)
        for i in range(4)
    ]
    block_out = project(order, own_sides, w_out, x_cols)[None]

    stacked = jnp.stack([r[:, :length] for r in rows])
    flat = stacked.transpose(0, 2, 1, 3).reshape(count * length, size * local)
    kernel_m = lax.dot_general(flat, flat, (((1,), (1,)), ((), ())), preferred_element_type=F32)
    if length <= local:
        slots = jnp.argsort(order)
        pieces = []
        for r in rows:
            part = r[:, length : length + share].astype(F32) + r[:, length + share :].astype(F32)
            pieces.append(part[slots].reshape(rank, local)[:, :length].T)
        weights = jnp.concatenate(pieces, axis=0)
    else:
        weights = jnp.concatenate(sequences(lax.psum(side, "fsdp").T, count), axis=0)
    product = jnp.dot(kernel_m, weights, precision=HIGH)
    gram = dot_high(weights, product, ((0,), (0,)))
    inverse = inverse_factor(gram) * jnp.sqrt(F32(size * local))
    y_both = jnp.concatenate([p[:length] for p in y_seqs], axis=0).astype(F32)
    panel = dot_high(y_both, weights, ((0,), (0,)))
    basis = dot_high(panel, inverse, ((1,), (1,))).astype(BF16)
    turned = dot_high(product, inverse, ((1,), (1,)))
    cot_both = jnp.concatenate(sequences(cot_cols, count), axis=0).astype(F32)
    right_raw = dot_high(cot_both, turned, ((0,), (0,)))
    column_sums = plane_sum(jnp.sum(right_raw * right_raw, axis=0, keepdims=True), size)
    right_factor = right_raw * lax.rsqrt(column_sums / (size * width) + 1e-06)

    norm_factor = 1.0 / jnp.sqrt(F32(count * length))
    terms = filter_taps(y_grad, qkv, saved, inner, feat_filter.shape[1]) * norm_factor
    halves = sequences(terms.astype(BF16), count)
    filter_grad = sum(h.astype(F32) for h in halves)
    return (block_out, filter_grad, basis, right_factor)


def finish_kernel(flag, order, *refs):
    count = len(RELATIVE)
    pieces = refs[:count]
    side_own, side_other, cot_own, cot_other, x, weights = refs[count : count + 6]
    block_out, basis, right_raw, sums = refs[count + 6 : count + 10]
    rows, cots, sides, inverse, here, sems = refs[count + 10 :]
    copies = copies_in(weights, here, sems)
    mine = flag[0]
    other = 1 - mine
    length = cots.shape[1]
    local = pieces[0].shape[1]
    for at, piece in enumerate(pieces):
        lanes = slice(at * local, (at + 1) * local)
        rows[mine, :, lanes] = piece[:length, :]
        rows[other, :, lanes] = piece[length:, :]
    sides[mine] = side_own[...]
    sides[other] = side_other[...]
    cots[mine] = cot_own[...]
    cots[other] = cot_other[...]
    turned = [sides[0], sides[1]]
    first, second = rows[0], rows[1]
    transposed = ((1,), (1,))
    plain = ((1,), (0,))
    soft = lambda a, b, contract: lax.dot_general(a, b, (contract, ((), ())), preferred_element_type=F32)
    corner = soft(first, first, transposed)
    across = soft(first, second, transposed)
    across_t = soft(second, first, transposed)
    end = soft(second, second, transposed)
    upper = dot_high(corner, turned[0], plain) + dot_high(across, turned[1], plain)
    under = dot_high(across_t, turned[0], plain) + dot_high(end, turned[1], plain)
    rowwise = ((0,), (0,))
    gram = dot_high(turned[0], upper, rowwise) + dot_high(turned[1], under, rowwise)
    for copy in copies:
        copy.wait()
    total = x[:length, :].astype(F32)
    for slot, piece in enumerate(pieces):
        place = pl.ds(pl.multiple_of(order[slot] * local, local), local)
        total = total + jnp.dot(piece[:length, :], here[place, :], preferred_element_type=F32)
    block_out[...] = total.astype(BF16)
    factor_kernel(gram, inverse)
    scaled = inverse[...] * math.sqrt(local * count)
    panel = jnp.zeros((local, gram.shape[0]), F32)
    for i in (0, 1):
        own = jnp.where(mine == i, pieces[0][:length, :], pieces[0][length:, :])
        top = turned[i].astype(BF16)
        rest = (turned[i] - top.astype(F32)).astype(BF16)
        panel = panel + soft(own, top, rowwise) + soft(own, rest, rowwise)
    basis[...] = dot_high(panel, scaled, transposed).astype(BF16)
    raw = jnp.zeros(right_raw.shape, F32)
    for i, product in enumerate((upper, under)):
        turn = dot_high(product, scaled, transposed)
        top = turn.astype(BF16)
        rest = (turn - top.astype(F32)).astype(BF16)
        raw = raw + soft(cots[i], top, ((0,), (0,))) + soft(cots[i], rest, ((0,), (0,)))
    right_raw[...] = raw
    sums[...] = jnp.sum(raw * raw, axis=0, keepdims=True)


def finish(flag, order, pieces, side_own, side_other, cot_own, cot_other, x, w_out):
    local = pieces[0].shape[1]
    length, width = cot_own.shape
    rank = side_own.shape[1]
    count = len(pieces)
    whole = pl.BlockSpec(memory_space=pltpu.VMEM)
    return pl.pallas_call(
        finish_kernel,
        out_shape=(
            jax.ShapeDtypeStruct((length, width), BF16),
            jax.ShapeDtypeStruct((local, rank), BF16),
            jax.ShapeDtypeStruct((width, rank), F32),
            jax.ShapeDtypeStruct((1, rank), F32),
        ),
        in_specs=[pl.BlockSpec(memory_space=pltpu.SMEM)] * 2
        + [whole] * (count + 5)
        + [pl.BlockSpec(memory_space=pltpu.HBM)],
        out_specs=(whole,) * 4,
        scratch_shapes=[
            pltpu.VMEM((2, length, count * local), BF16),
            pltpu.VMEM((2, length, width), BF16),
            pltpu.VMEM((2, length, rank), F32),
            pltpu.VMEM((rank, rank), F32),
            pltpu.VMEM(w_out.shape, w_out.dtype),
            pltpu.SemaphoreType.DMA((8,)),
        ],
        compiler_params=pltpu.CompilerParams(vmem_limit_bytes=20 * 2**20),
        cost_estimate=pl.CostEstimate(flops=2**33, transcendentals=0, bytes_accessed=2**22),
        name="finish",
    )(flag, order, *pieces, side_own, side_other, cot_own, cot_other, x, w_out)


FREE = pl.CostEstimate(flops=1, transcendentals=0, bytes_accessed=1)


def copies_in(source, target, sems):
    count = sems.shape[0]
    rows = source.shape[0] // count
    copies = []
    for i in range(count):
        part = pl.ds(i * rows, rows)
        copies.append(pltpu.make_async_copy(source.at[part], target.at[part], sems.at[i]))
        copies[-1].start()
    return copies


def parts_kernel(order, weights, cot, send, keep, here, sems, *, local):
    half = send.shape[0]
    for copy in copies_in(weights, here, sems):
        copy.wait()
    for slot in range(2 * half):
        out, at = (send, slot) if slot < half else (keep, slot - half)
        rows = here[pl.ds(pl.multiple_of(order[slot] * local, local), local), :]
        out[at] = lax.dot_general(
            cot[...], rows, (((1,), (1,)), ((), ())), preferred_element_type=F32
        ).astype(BF16)


def grad_parts(order, w_out, cot, size):
    length = cot.shape[0]
    local, half = w_out.shape[0] // size, size // 2
    shape = jax.ShapeDtypeStruct((half, length, local), BF16)
    whole = pl.BlockSpec(memory_space=pltpu.VMEM)
    return pl.pallas_call(
        functools.partial(parts_kernel, local=local),
        out_shape=(shape, shape),
        in_specs=[pl.BlockSpec(memory_space=pltpu.SMEM), pl.BlockSpec(memory_space=pltpu.HBM), whole],
        out_specs=(whole, whole),
        scratch_shapes=[pltpu.VMEM(w_out.shape, w_out.dtype), pltpu.SemaphoreType.DMA((8,))],
        compiler_params=pltpu.CompilerParams(vmem_limit_bytes=16 * 2**20),
        cost_estimate=FREE,
        name="grad_parts",
    )(order, w_out, cot)


RELATIVE = (0, 2, 4, 6, 8, 10, 12, 14, 1, 3, 5, 7, 9, 11, 13, 15)


def mix_whole_kernel(order, *refs, length):
    count = len(RELATIVE)
    pieces, weights = refs[:count], refs[count]
    feat, inner = refs[count + 1 : count + 3]
    y_out, qkv_out, saved = refs[count + 3 : count + 6]
    normed, pad, here, sems = refs[count + 6 :]
    copies = [copies_in(weights.at[i], here.at[i], sems.at[i]) for i in range(3)]
    taps = inner.shape[0]
    step = pieces[0].shape[1]
    squares = jnp.zeros((length, step), F32)
    for piece in pieces:
        a = piece[:length, :].astype(F32)
        squares = squares + a * a
    scale = lax.rsqrt(jnp.sum(squares, axis=1, keepdims=True) / (step * count) + 1e-05)
    for slot, piece in enumerate(pieces):
        place = pl.ds(pl.multiple_of(order[slot] * step, step), step)
        gain = piece[length:, :][0:1].astype(F32)
        normed[:, place] = (piece[:length, :].astype(F32) * scale * gain).astype(BF16)
    convs = []
    for which in range(3):
        for copy in copies[which]:
            copy.wait()
        half = lax.dot_general(
            normed[...], here[which], (((1,), (1,)), ((), ())), preferred_element_type=F32
        ).astype(BF16)
        qkv_out[which] = half
        pad_front(pad, half.astype(F32))
        result = jnp.zeros(half.shape, F32)
        for lag in range(taps):
            result = result + feat[which, lag : lag + 1, :] * lagged(pad, lag, length)
        convs.append(result)
        saved[which] = result
    gated = convs[1] * convs[2]
    saved[3] = gated
    pad_front(pad, gated)
    window = jnp.zeros(gated.shape, F32)
    for lag in range(taps):
        window = window + inner[lag : lag + 1, :] * lagged(pad, lag, length)
    saved[4] = window
    y_out[...] = (convs[0] * window).astype(BF16)


def mix_whole(order, pieces, w_in, feat, inner):
    rows, step = pieces[0].shape
    length = rows - EXTRA
    local, width = w_in.shape[1:]
    whole = pl.BlockSpec(memory_space=pltpu.VMEM)
    return pl.pallas_call(
        functools.partial(mix_whole_kernel, length=length),
        out_shape=(
            jax.ShapeDtypeStruct((length, local), BF16),
            jax.ShapeDtypeStruct((3, length, local), BF16),
            jax.ShapeDtypeStruct((5, length, local), F32),
        ),
        in_specs=[pl.BlockSpec(memory_space=pltpu.SMEM)]
        + [whole] * len(pieces)
        + [pl.BlockSpec(memory_space=pltpu.HBM), whole, whole],
        out_specs=(whole, whole, whole),
        scratch_shapes=[
            pltpu.VMEM((length, width), BF16),
            pltpu.VMEM((length + 16, local), F32),
            pltpu.VMEM(w_in.shape, w_in.dtype),
            pltpu.SemaphoreType.DMA((3, 1)),
        ],
        compiler_params=pltpu.CompilerParams(vmem_limit_bytes=24 * 2**20),
        cost_estimate=pl.CostEstimate(
            flops=6 * length * local * width, transcendentals=0, bytes_accessed=6 * local * width
        ),
        name="mix",
    )(order, *pieces, w_in, feat, inner)


def after(value, *events):
    return lax.optimization_barrier((value,) + events)[0]


def terms_kernel(summed, qkv, saved, inner, pool, out, pad, stack, sums, *, scale):
    taps_kernel(summed, qkv, saved, inner, pool, sums, pad, stack)
    out[...] = (sums[...] * scale).astype(BF16)


def filter_terms(summed, qkv, saved, inner, groups, scale):
    length, local = qkv.shape[1:]
    member = jnp.arange(local)[:, None] // (local // groups) == jnp.arange(groups)[None, :]
    return pl.pallas_call(
        functools.partial(terms_kernel, scale=scale),
        out_shape=jax.ShapeDtypeStruct((32, groups), BF16),
        scratch_shapes=[
            pltpu.VMEM((length + 16, local), F32),
            pltpu.VMEM((32, local), F32),
            pltpu.VMEM((32, groups), F32),
        ],
        cost_estimate=FREE,
        name="filter_terms",
    )(summed, qkv, saved, inner, member.astype(F32))


def hop_all(piece, size):
    send = functools.partial(exchange, axis="fsdp", size=size)
    have = {0: piece}
    for z in (4, 8, 12):
        have[z] = send(piece, bits=z)
    for z in (0, 4, 8, 12):
        have[z + 2] = send(have[z], bits=2)
    for near in (0, 4, 2, 6, 8, 10, 12, 14):
        have[near + 1] = send(have[near], bits=1)
    return have


def both_ways(value, bits, size):
    half = value.astype(BF16)
    return half.astype(F32) + exchange(half, "fsdp", size, bits).astype(F32)


def tuned_device(ids, embed, gain, w_in, feat_filter, inner_filter, w_out, cotangent, right_prev):
    size = lax.axis_size("fsdp")
    count = lax.axis_size("dp")
    tokens = ids[0]
    length = tokens.shape[0]
    vocab, width = embed.shape
    local = w_in.shape[1]
    rank = right_prev.shape[1]
    index = lax.axis_index("fsdp").astype(jnp.int32)
    order = jnp.bitwise_xor(index, jnp.array(RELATIVE, jnp.int32))
    flag = lax.axis_index("dp").astype(jnp.int32)[None]
    send = functools.partial(exchange, axis="fsdp", size=size)
    feat = spread(feat_filter, local)
    inner = spread(inner_filter, local)

    onehot = (tokens[:, None] == jnp.arange(vocab, dtype=jnp.int32)[None, :]).astype(BF16)
    x_cols = jnp.dot(onehot, embed, preferred_element_type=F32).astype(BF16)
    x_sent = jnp.concatenate([x_cols, jnp.broadcast_to(gain[None, :], (EXTRA, width))], axis=0)
    have = hop_all(x_sent, size)
    w_in = pltpu.with_memory_space_constraint(w_in, pltpu.HBM)
    w_out = pltpu.with_memory_space_constraint(w_out, pltpu.HBM)

    cot_cols = cotangent[0]
    turns = [c + x + f + n for c in (1, 0) for x in (2, 0) for f in (8, 0) for n in (4, 0)]
    targets = jnp.bitwise_xor(index, jnp.array(turns, jnp.int32))
    away, keep = grad_parts(targets, w_out, cot_cols, size)
    keep = keep.astype(F32) + send(away, bits=1).astype(F32)
    away, keep = keep[:4].astype(BF16), keep[4:]
    side = jnp.dot(cot_cols, right_prev, preferred_element_type=F32)
    side = both_ways(side, 1, size)
    ready = after(order, side, away, keep)
    y, qkv, saved = mix_whole(ready, [have[r] for r in RELATIVE], w_in, feat, inner)

    keep = keep + send(away, bits=2).astype(F32)
    keep = keep[2:] + send(keep[:2].astype(BF16), bits=8).astype(F32)
    y_grad = (keep[1:] + send(keep[:1].astype(BF16), bits=4).astype(F32))[0]
    for bits in (2, 4, 8):
        side = both_ways(side, bits, size)
    side_other = exchange(side, "dp", count, 1)

    y_other = exchange(y, "dp", count, 1)
    got = hop_all(jnp.concatenate([y, y_other], axis=0), size)
    cot_other = exchange(after(cot_cols, got[4]), "dp", count, 1)
    groups = feat_filter.shape[1]
    scale = 1.0 / math.sqrt(count * length)
    terms = filter_terms(after(y_grad, got[12]), qkv, saved, inner, groups, scale)
    terms_other = exchange(terms, "dp", count, 1)
    filter_grad = terms.astype(F32) + terms_other.astype(F32)
    filter_grad = jnp.swapaxes(filter_grad.reshape(4, 8, groups), 1, 2)[:, :, : inner.shape[0]]
    got[15] = send(after(got[14], terms), bits=1)
    pieces = [got[r] for r in RELATIVE]
    block_out, basis, right_raw, sums = finish(
        flag, order, pieces, side, side_other, cot_cols, cot_other, x_sent, w_out
    )
    column_sums = plane_sum(sums, size)
    right_factor = right_raw * lax.rsqrt(column_sums / (size * width) + 1e-06)
    return (block_out[None], filter_grad, basis, right_factor)


def per_device(ids, embed, gain, w_in, feat_filter, inner_filter, w_out, cotangent, right_prev):
    sizes = (lax.axis_size("dp"), lax.axis_size("fsdp"))
    shapes = (ids.shape[1], w_in.shape[1], right_prev.shape[1])
    body = tuned_device if sizes == (2, 16) and shapes == (192, 256, 256) else general_device
    return body(ids, embed, gain, w_in, feat_filter, inner_filter, w_out, cotangent, right_prev)


def solution(mesh):
    placed = (
        P("dp", None),
        P(None, "fsdp"),
        P("fsdp"),
        P(None, "fsdp", None),
        P(None, "fsdp", None),
        P("fsdp", None),
        P(None, "fsdp"),
        P("dp", None, "fsdp"),
        P("fsdp", None),
    )
    return jax.shard_map(
        per_device,
        mesh=mesh,
        in_specs=placed,
        out_specs=(P("dp", None, "fsdp"), P(None, "fsdp", None), P("fsdp", None), P("fsdp", None)),
        check_vma=False,
    )
```

```python
import functools
import math

import jax
import jax.numpy as jnp
from jax import lax
from jax.experimental import pallas as pl
from jax.experimental.pallas import tpu as pltpu
from jax.sharding import PartitionSpec as P

HIGH = lax.Precision.HIGHEST
F32 = jnp.float32
BF16 = jnp.bfloat16
EXTRA = 16


def exchange(value, axis, size, bits):
    return lax.ppermute(value, axis, [(i, i ^ bits) for i in range(size)])


def plane_gather(piece, size):
    if size != 16:
        whole = lax.all_gather(piece, "fsdp", axis=0)
        quarter = size // 4
        return [whole[i * quarter : (i + 1) * quarter] for i in range(4)]
    send = functools.partial(exchange, axis="fsdp", size=size)
    line = jnp.stack([piece] + [send(piece, bits=4 * step) for step in (1, 2, 3)])
    across = send(line, bits=2)
    return [line, across, send(line, bits=1), send(across, bits=1)]


def plane_order(size):
    if size != 16:
        return jnp.arange(size, dtype=jnp.int32)
    index = lax.axis_index("fsdp").astype(jnp.int32)
    slots = [(bit_x * 2 + bit_core) ^ (4 * step) for bit_core in (0, 1) for bit_x in (0, 1) for step in range(4)]
    return jnp.bitwise_xor(index, jnp.array(slots, jnp.int32))


def plane_sum(value, size):
    if size != 16:
        return lax.psum(value, "fsdp")
    send = functools.partial(exchange, axis="fsdp", size=size)
    value = value + send(value, bits=1)
    value = value + send(value, bits=2)
    value = value + send(value, bits=4)
    return value + send(value, bits=8)


def plane_scatter(parts, size):
    index = lax.axis_index("fsdp")
    if size != 16:
        return lax.psum_scatter(parts.astype(F32), "fsdp", scatter_dimension=0, tiled=True)[0]
    rows = parts.shape[1:]
    for bits, lead in ((1, 8), (2, 4), (8, 1), (4, 1)):
        if bits < 4:
            view = parts.reshape((lead, 2) + rows)
            axis, own = 1, (index // bits) % 2
        else:
            count = parts.shape[0]
            view = parts.reshape((2, count // 2) + rows)
            axis, own = 0, (index // bits) % 2
        sent = lax.dynamic_index_in_dim(view, 1 - own, axis, keepdims=False).astype(BF16)
        kept = lax.dynamic_index_in_dim(view, own, axis, keepdims=False).astype(F32)
        parts = kept + exchange(sent, "fsdp", size, bits).astype(F32)
    return parts[0]


def sequences(value, count):
    if count != 2:
        gathered = lax.all_gather(value, "dp", axis=0)
        return [gathered[i] for i in range(count)]
    other = exchange(value, "dp", count, 1)
    first = lax.axis_index("dp") == 0
    return [jnp.where(first, value, other), jnp.where(first, other, value)]


def spread(table, width):
    group = width // table.shape[-2]
    return jnp.repeat(jnp.swapaxes(table, -1, -2), group, axis=-1)


def pad_front(pad, signal):
    length = signal.shape[0]
    pad[pl.ds(0, 8), :] = jnp.zeros((8, signal.shape[1]), F32)
    pad[pl.ds(8, length), :] = signal


def lagged(pad, lag, length):
    return pad[pl.ds(8 - lag, length), :]


def mix_kernel(order, *refs, length, cut, width):
    early, late, weights = refs[0:4], refs[4:8], refs[8:12]
    feat, inner = refs[12:14]
    y_out, qkv_out, saved = refs[14:17]
    acc, factor, pad = refs[17:20]
    step = pl.program_id(0)
    taps = inner.shape[0]

    @pl.when(step == 0)
    def _():
        top = jnp.zeros((cut, 1), F32)
        low = jnp.zeros((length - cut, 1), F32)
        for slot in range(early[0].shape[0]):
            for side in range(4):
                a = early[side][slot].astype(F32)
                b = late[side][slot, : length - cut, :].astype(F32)
                top = top + jnp.sum(a * a, axis=1, keepdims=True)
                low = low + jnp.sum(b * b, axis=1, keepdims=True)
        squares = jnp.concatenate([top, low], axis=0)
        factor[...] = jnp.broadcast_to(lax.rsqrt(squares / width + 1e-05), factor.shape)
        acc[...] = jnp.zeros_like(acc)

    scale = factor[:, 0:1]
    for side in range(4):
        gain = late[side][step, pl.ds(length - cut, EXTRA), :][0:1].astype(F32)
        a = early[side][step].astype(F32)
        b = late[side][step, pl.ds(0, length - cut), :].astype(F32)
        normed = (jnp.concatenate([a, b], axis=0) * scale * gain).astype(BF16)
        for which in range(3):
            acc[which] += lax.dot_general(
                normed, weights[side][which], (((1,), (1,)), ((), ())), preferred_element_type=F32
            )

    @pl.when(step == pl.num_programs(0) - 1)
    def _():
        convs = []
        for which in range(3):
            half = acc[which].astype(BF16)
            qkv_out[which] = half
            pad_front(pad, half.astype(F32))
            total = jnp.zeros((length, acc.shape[2]), F32)
            for lag in range(taps):
                total = total + feat[which, lag : lag + 1, :] * lagged(pad, lag, length)
            convs.append(total)
            saved[which] = total
        gated = convs[1] * convs[2]
        saved[3] = gated
        pad_front(pad, gated)
        window = jnp.zeros(gated.shape, F32)
        for lag in range(taps):
            window = window + inner[lag : lag + 1, :] * lagged(pad, lag, length)
        saved[4] = window
        y_out[...] = (convs[0] * window).astype(BF16)


def mix(order, early, late, w_in, feat, inner):
    slots, cut, width = early[0].shape
    length = cut + late[0].shape[1] - EXTRA
    local = w_in.shape[1]
    taps = inner.shape[0]
    full = lambda shape: pl.BlockSpec(shape, lambda i, o: (0,) * len(shape))
    weight = lambda side: pl.BlockSpec((3, local, width), lambda i, o: (0, 0, o[side * slots + i]))
    return pl.pallas_call(
        functools.partial(mix_kernel, length=length, cut=cut, width=w_in.shape[2]),
        out_shape=(
            jax.ShapeDtypeStruct((length, local), BF16),
            jax.ShapeDtypeStruct((3, length, local), BF16),
            jax.ShapeDtypeStruct((5, length, local), F32),
        ),
        grid_spec=pltpu.PrefetchScalarGridSpec(
            num_scalar_prefetch=1,
            grid=(slots,),
            in_specs=[full(e.shape) for e in early]
            + [full(e.shape) for e in late]
            + [weight(side) for side in range(4)]
            + [full(feat.shape), full(inner.shape)],
            out_specs=(full((length, local)), full((3, length, local)), full((5, length, local))),
            scratch_shapes=[
                pltpu.VMEM((3, length, local), F32),
                pltpu.VMEM((length, 128), F32),
                pltpu.VMEM((length + 16, local), F32),
            ],
        ),
        compiler_params=pltpu.CompilerParams(
            dimension_semantics=("arbitrary",), vmem_limit_bytes=48 * 2**20
        ),
        name="mix",
    )(order, *early, *late, w_in, w_in, w_in, w_in, feat, inner)


def taps_kernel(grad, qkv, saved, inner, pool, out, pad, stack):
    length = grad.shape[0]
    taps = inner.shape[0]
    given = grad[...]
    query_conv, key_conv, value_conv = saved[0], saved[1], saved[2]
    query_grad = given * saved[4]
    window_grad = given * query_conv
    pad[pl.ds(0, length), :] = window_grad
    pad[pl.ds(length, 8), :] = jnp.zeros((8, given.shape[1]), F32)
    gated_grad = jnp.zeros(given.shape, F32)
    for lag in range(taps):
        gated_grad = gated_grad + inner[lag : lag + 1, :] * pad[pl.ds(lag, length), :]
    pairs = (
        (query_grad, qkv[0].astype(F32)),
        (gated_grad * value_conv, qkv[1].astype(F32)),
        (gated_grad * key_conv, qkv[2].astype(F32)),
        (window_grad, saved[3]),
    )
    stack[...] = jnp.zeros_like(stack)
    for row, (gradient, signal) in enumerate(pairs):
        pad_front(pad, signal)
        for lag in range(taps):
            stack[8 * row + lag : 8 * row + lag + 1, :] = jnp.sum(
                gradient * lagged(pad, lag, length), axis=0, keepdims=True
            )
    out[...] = lax.dot_general(
        stack[...], pool[...], (((1,), (0,)), ((), ())), precision=HIGH, preferred_element_type=F32
    )


def filter_taps(grad, qkv, saved, inner, groups):
    length, local = grad.shape
    member = jnp.arange(local)[:, None] // (local // groups) == jnp.arange(groups)[None, :]
    out = pl.pallas_call(
        taps_kernel,
        out_shape=jax.ShapeDtypeStruct((32, groups), F32),
        scratch_shapes=[pltpu.VMEM((length + 16, local), F32), pltpu.VMEM((32, local), F32)],
        name="filter_taps",
    )(grad, qkv, saved, inner, member.astype(F32))
    return jnp.swapaxes(out.reshape(4, 8, groups), 1, 2)[:, :, : inner.shape[0]]


def out_kernel(order, *refs, length):
    sides, weights, x, out, acc = refs[0:4], refs[4:8], refs[8], refs[9], refs[10]
    step = pl.program_id(0)

    @pl.when(step == 0)
    def _():
        acc[...] = jnp.zeros_like(acc)

    total = acc[...]
    for side in range(4):
        total = total + jnp.dot(
            sides[side][0, :length, :], weights[side][...], preferred_element_type=F32
        )
    acc[...] = total

    @pl.when(step == pl.num_programs(0) - 1)
    def _():
        out[...] = (x[...].astype(F32) + total).astype(BF16)


def project(order, sides, w_out, x):
    length, width = x.shape
    slots, rows, local = sides[0].shape
    full = lambda shape: pl.BlockSpec(shape, lambda i, o: (0,) * len(shape))
    weight = lambda side: pl.BlockSpec((local, width), lambda i, o: (o[side * slots + i], 0))
    return pl.pallas_call(
        functools.partial(out_kernel, length=length),
        out_shape=jax.ShapeDtypeStruct((length, width), BF16),
        grid_spec=pltpu.PrefetchScalarGridSpec(
            num_scalar_prefetch=1,
            grid=(slots,),
            in_specs=[pl.BlockSpec((1, rows, local), lambda i, o: (i, 0, 0)) for _ in range(4)]
            + [weight(side) for side in range(4)]
            + [full((length, width))],
            out_specs=full((length, width)),
            scratch_shapes=[pltpu.VMEM((length, width), F32)],
        ),
        compiler_params=pltpu.CompilerParams(dimension_semantics=("arbitrary",)),
        name="project",
    )(order, *sides, w_out, w_out, w_out, w_out, x)


def eliminate(block):
    size = block.shape[0]
    row = lax.broadcasted_iota(jnp.int32, (size, size), 0)
    lane = lax.broadcasted_iota(jnp.int32, (size, size), 1)
    unit = (row == lane).astype(F32)
    left = [block[8 * i : 8 * i + 8, :] for i in range(size // 8)]
    right = [unit[8 * i : 8 * i + 8, :] for i in range(size // 8)]
    inside = lax.broadcasted_iota(jnp.int32, (8, size), 0)
    wide = lambda tile, j: jnp.broadcast_to(tile[:, j : j + 1], (8, size))
    for at in range(size // 8):
        a, v = left[at], right[at]
        cols = [wide(a, 8 * at + k) for k in range(8)]
        inverses = []
        for k in range(8):
            inverse = 1.0 / cols[k][k : k + 1, :]
            inverses.append(inverse)
            share = jnp.where(inside > k, cols[k] * inverse, 0.0)
            for l in range(k + 1, 8):
                cols[l] = cols[l] - share * cols[l][k : k + 1, :]
            a = a - share * a[k : k + 1, :]
            v = v - share * v[k : k + 1, :]
        left[at], right[at] = a, v
        for i in range(at + 1, size // 8):
            mine = [wide(left[i], 8 * at + k) for k in range(8)]
            p, q = left[i], right[i]
            for k in range(8):
                share = mine[k] * inverses[k]
                for l in range(k + 1, 8):
                    mine[l] = mine[l] - share * cols[l][k : k + 1, :]
                p = p - share * a[k : k + 1, :]
                q = q - share * v[k : k + 1, :]
            left[i], right[i] = p, q
    upper = jnp.concatenate(left, axis=0)
    diagonal = jnp.sum(jnp.where(row == lane, upper, 0.0), axis=1, keepdims=True)
    return jnp.concatenate(right, axis=0) * lax.rsqrt(diagonal)


def dot_high(a, b, contract):
    return lax.dot_general(a, b, (contract, ((), ())), precision=HIGH, preferred_element_type=F32)


def factor_kernel(gram, out):
    half = gram.shape[0] // 2
    first = eliminate(gram[:half, :half])
    below = dot_high(gram[half:, :half], first, ((1,), (1,)))
    rest = gram[half:, half:] - dot_high(below, below, ((1,), (1,)))
    second = eliminate(rest)
    corner = -dot_high(second, dot_high(below, first, ((1,), (0,))), ((1,), (0,)))
    out[:half, :half] = first
    out[:half, half:] = jnp.zeros((half, half), F32)
    out[half:, :half] = corner
    out[half:, half:] = second


def inverse_factor(gram):
    return pl.pallas_call(
        factor_kernel,
        out_shape=jax.ShapeDtypeStruct(gram.shape, F32),
        name="inverse_factor",
    )(gram)


def general_device(ids, embed, gain, w_in, feat_filter, inner_filter, w_out, cotangent, right_prev):
    size = lax.axis_size("fsdp")
    count = lax.axis_size("dp")
    tokens = ids[0]
    length = tokens.shape[0]
    vocab, width = embed.shape
    local = w_in.shape[1]
    rank = right_prev.shape[1]
    cut = length // 2
    order = plane_order(size)

    onehot = (tokens[:, None] == jnp.arange(vocab, dtype=jnp.int32)[None, :]).astype(BF16)
    x_cols = jnp.dot(onehot, embed, preferred_element_type=F32).astype(BF16)
    tail = jnp.broadcast_to(gain[None, :], (EXTRA, width))
    early = plane_gather(x_cols[:cut], size)
    late = plane_gather(jnp.concatenate([x_cols[cut:], tail], axis=0), size)

    cot_cols = cotangent[0]
    parts = jnp.einsum(
        "scd,ld->slc", w_out.reshape(size, local, width), cot_cols, preferred_element_type=F32
    ).astype(BF16)
    side = lax.dot_general(right_prev, cot_cols, (((0,), (1,)), ((), ())), preferred_element_type=F32)
    share = rank // size
    if length <= local:
        packed = jnp.pad(side, ((0, 0), (0, local - length))).reshape(size, share, local)
        summed = plane_scatter(jnp.concatenate([parts, packed.astype(BF16)], axis=1), size)
        y_grad = summed[:length]
        side_own = summed[length:]
        high = side_own.astype(BF16)
        low = (side_own - high.astype(F32)).astype(BF16)
        rider = jnp.concatenate([high, low], axis=0)
    else:
        y_grad = plane_scatter(parts, size)
        rider = jnp.zeros((0, local), BF16)

    feat = spread(feat_filter, local)
    inner = spread(inner_filter, local)
    y, qkv, saved = mix(order, early, late, w_in, feat, inner)

    sent = jnp.concatenate([y, rider], axis=0)
    y_seqs = sequences(sent, count)
    gathered = [plane_gather(piece, size) for piece in y_seqs]
    rows = [jnp.concatenate(sides, axis=0) for sides in gathered]
    mine = lax.axis_index("dp")
    own_sides = [
        lax.dynamic_index_in_dim(jnp.stack([g[i] for g in gathered]), mine, 0, keepdims=False)
        for i in range(4)
    ]
    block_out = project(order, own_sides, w_out, x_cols)[None]

    stacked = jnp.stack([r[:, :length] for r in rows])
    flat = stacked.transpose(0, 2, 1, 3).reshape(count * length, size * local)
    kernel_m = lax.dot_general(flat, flat, (((1,), (1,)), ((), ())), preferred_element_type=F32)
    if length <= local:
        slots = jnp.argsort(order)
        pieces = []
        for r in rows:
            part = r[:, length : length + share].astype(F32) + r[:, length + share :].astype(F32)
            pieces.append(part[slots].reshape(rank, local)[:, :length].T)
        weights = jnp.concatenate(pieces, axis=0)
    else:
        weights = jnp.concatenate(sequences(lax.psum(side, "fsdp").T, count), axis=0)
    product = jnp.dot(kernel_m, weights, precision=HIGH)
    gram = dot_high(weights, product, ((0,), (0,)))
    inverse = inverse_factor(gram) * jnp.sqrt(F32(size * local))
    y_both = jnp.concatenate([p[:length] for p in y_seqs], axis=0).astype(F32)
    panel = dot_high(y_both, weights, ((0,), (0,)))
    basis = dot_high(panel, inverse, ((1,), (1,))).astype(BF16)
    turned = dot_high(product, inverse, ((1,), (1,)))
    cot_both = jnp.concatenate(sequences(cot_cols, count), axis=0).astype(F32)
    right_raw = dot_high(cot_both, turned, ((0,), (0,)))
    column_sums = plane_sum(jnp.sum(right_raw * right_raw, axis=0, keepdims=True), size)
    right_factor = right_raw * lax.rsqrt(column_sums / (size * width) + 1e-06)

    norm_factor = 1.0 / jnp.sqrt(F32(count * length))
    terms = filter_taps(y_grad, qkv, saved, inner, feat_filter.shape[1]) * norm_factor
    halves = sequences(terms.astype(BF16), count)
    filter_grad = sum(h.astype(F32) for h in halves)
    return (block_out, filter_grad, basis, right_factor)


def finish_kernel(flag, order, *refs):
    count = len(RELATIVE)
    pieces = refs[:count]
    side_own, side_other, cot_own, cot_other, x, weights = refs[count : count + 6]
    block_out, basis, right_raw, sums = refs[count + 6 : count + 10]
    rows, cots, sides, inverse, here, sems = refs[count + 10 :]
    copies = copies_in(weights, here, sems)
    mine = flag[0]
    other = 1 - mine
    length = cots.shape[1]
    local = pieces[0].shape[1]
    for at, piece in enumerate(pieces):
        lanes = slice(at * local, (at + 1) * local)
        rows[mine, :, lanes] = piece[:length, :]
        rows[other, :, lanes] = piece[length:, :]
    sides[mine] = side_own[...]
    sides[other] = side_other[...]
    cots[mine] = cot_own[...]
    cots[other] = cot_other[...]
    turned = [sides[0], sides[1]]
    first, second = rows[0], rows[1]
    transposed = ((1,), (1,))
    plain = ((1,), (0,))
    soft = lambda a, b, contract: lax.dot_general(a, b, (contract, ((), ())), preferred_element_type=F32)
    corner = soft(first, first, transposed)
    across = soft(first, second, transposed)
    across_t = soft(second, first, transposed)
    end = soft(second, second, transposed)
    upper = dot_high(corner, turned[0], plain) + dot_high(across, turned[1], plain)
    under = dot_high(across_t, turned[0], plain) + dot_high(end, turned[1], plain)
    rowwise = ((0,), (0,))
    gram = dot_high(turned[0], upper, rowwise) + dot_high(turned[1], under, rowwise)
    for copy in copies:
        copy.wait()
    total = x[:length, :].astype(F32)
    for slot, piece in enumerate(pieces):
        place = pl.ds(pl.multiple_of(order[slot] * local, local), local)
        total = total + jnp.dot(piece[:length, :], here[place, :], preferred_element_type=F32)
    block_out[...] = total.astype(BF16)
    factor_kernel(gram, inverse)
    scaled = inverse[...] * math.sqrt(local * count)
    panel = jnp.zeros((local, gram.shape[0]), F32)
    for i in (0, 1):
        own = jnp.where(mine == i, pieces[0][:length, :], pieces[0][length:, :])
        top = turned[i].astype(BF16)
        rest = (turned[i] - top.astype(F32)).astype(BF16)
        panel = panel + soft(own, top, rowwise) + soft(own, rest, rowwise)
    basis[...] = dot_high(panel, scaled, transposed).astype(BF16)
    raw = jnp.zeros(right_raw.shape, F32)
    for i, product in enumerate((upper, under)):
        turn = dot_high(product, scaled, transposed)
        top = turn.astype(BF16)
        rest = (turn - top.astype(F32)).astype(BF16)
        raw = raw + soft(cots[i], top, ((0,), (0,))) + soft(cots[i], rest, ((0,), (0,)))
    right_raw[...] = raw
    sums[...] = jnp.sum(raw * raw, axis=0, keepdims=True)


def finish(flag, order, pieces, side_own, side_other, cot_own, cot_other, x, w_out):
    local = pieces[0].shape[1]
    length, width = cot_own.shape
    rank = side_own.shape[1]
    count = len(pieces)
    whole = pl.BlockSpec(memory_space=pltpu.VMEM)
    return pl.pallas_call(
        finish_kernel,
        out_shape=(
            jax.ShapeDtypeStruct((length, width), BF16),
            jax.ShapeDtypeStruct((local, rank), BF16),
            jax.ShapeDtypeStruct((width, rank), F32),
            jax.ShapeDtypeStruct((1, rank), F32),
        ),
        in_specs=[pl.BlockSpec(memory_space=pltpu.SMEM)] * 2
        + [whole] * (count + 5)
        + [pl.BlockSpec(memory_space=pltpu.HBM)],
        out_specs=(whole,) * 4,
        scratch_shapes=[
            pltpu.VMEM((2, length, count * local), BF16),
            pltpu.VMEM((2, length, width), BF16),
            pltpu.VMEM((2, length, rank), F32),
            pltpu.VMEM((rank, rank), F32),
            pltpu.VMEM(w_out.shape, w_out.dtype),
            pltpu.SemaphoreType.DMA((8,)),
        ],
        compiler_params=pltpu.CompilerParams(vmem_limit_bytes=20 * 2**20),
        cost_estimate=pl.CostEstimate(flops=2**33, transcendentals=0, bytes_accessed=2**22),
        name="finish",
    )(flag, order, *pieces, side_own, side_other, cot_own, cot_other, x, w_out)


FREE = pl.CostEstimate(flops=1, transcendentals=0, bytes_accessed=1)


def copies_in(source, target, sems):
    count = sems.shape[0]
    rows = source.shape[0] // count
    copies = []
    for i in range(count):
        part = pl.ds(i * rows, rows)
        copies.append(pltpu.make_async_copy(source.at[part], target.at[part], sems.at[i]))
        copies[-1].start()
    return copies


def parts_kernel(order, weights, cot, send, keep, here, sems, *, local):
    half = send.shape[0]
    for copy in copies_in(weights, here, sems):
        copy.wait()
    for slot in range(2 * half):
        out, at = (send, slot) if slot < half else (keep, slot - half)
        rows = here[pl.ds(pl.multiple_of(order[slot] * local, local), local), :]
        out[at] = lax.dot_general(
            cot[...], rows, (((1,), (1,)), ((), ())), preferred_element_type=F32
        ).astype(BF16)


def grad_parts(order, w_out, cot, size):
    length = cot.shape[0]
    local, half = w_out.shape[0] // size, size // 2
    shape = jax.ShapeDtypeStruct((half, length, local), BF16)
    whole = pl.BlockSpec(memory_space=pltpu.VMEM)
    return pl.pallas_call(
        functools.partial(parts_kernel, local=local),
        out_shape=(shape, shape),
        in_specs=[pl.BlockSpec(memory_space=pltpu.SMEM), pl.BlockSpec(memory_space=pltpu.HBM), whole],
        out_specs=(whole, whole),
        scratch_shapes=[pltpu.VMEM(w_out.shape, w_out.dtype), pltpu.SemaphoreType.DMA((8,))],
        compiler_params=pltpu.CompilerParams(vmem_limit_bytes=16 * 2**20),
        cost_estimate=FREE,
        name="grad_parts",
    )(order, w_out, cot)


RELATIVE = (0, 2, 4, 6, 8, 10, 12, 14, 1, 3, 5, 7, 9, 11, 13, 15)


def mix_whole_kernel(order, *refs, length):
    count = len(RELATIVE)
    pieces, weights = refs[:count], refs[count]
    feat, inner = refs[count + 1 : count + 3]
    y_out, qkv_out, saved = refs[count + 3 : count + 6]
    normed, pad, here, sems = refs[count + 6 :]
    copies = [copies_in(weights.at[i], here.at[i], sems.at[i]) for i in range(3)]
    taps = inner.shape[0]
    step = pieces[0].shape[1]
    squares = jnp.zeros((length, step), F32)
    for piece in pieces:
        a = piece[:length, :].astype(F32)
        squares = squares + a * a
    scale = lax.rsqrt(jnp.sum(squares, axis=1, keepdims=True) / (step * count) + 1e-05)
    for slot, piece in enumerate(pieces):
        place = pl.ds(pl.multiple_of(order[slot] * step, step), step)
        gain = piece[length:, :][0:1].astype(F32)
        normed[:, place] = (piece[:length, :].astype(F32) * scale * gain).astype(BF16)
    convs = []
    for which in range(3):
        for copy in copies[which]:
            copy.wait()
        half = lax.dot_general(
            normed[...], here[which], (((1,), (1,)), ((), ())), preferred_element_type=F32
        ).astype(BF16)
        qkv_out[which] = half
        pad_front(pad, half.astype(F32))
        result = jnp.zeros(half.shape, F32)
        for lag in range(taps):
            result = result + feat[which, lag : lag + 1, :] * lagged(pad, lag, length)
        convs.append(result)
        saved[which] = result
    gated = convs[1] * convs[2]
    saved[3] = gated
    pad_front(pad, gated)
    window = jnp.zeros(gated.shape, F32)
    for lag in range(taps):
        window = window + inner[lag : lag + 1, :] * lagged(pad, lag, length)
    saved[4] = window
    y_out[...] = (convs[0] * window).astype(BF16)


def mix_whole(order, pieces, w_in, feat, inner):
    rows, step = pieces[0].shape
    length = rows - EXTRA
    local, width = w_in.shape[1:]
    whole = pl.BlockSpec(memory_space=pltpu.VMEM)
    return pl.pallas_call(
        functools.partial(mix_whole_kernel, length=length),
        out_shape=(
            jax.ShapeDtypeStruct((length, local), BF16),
            jax.ShapeDtypeStruct((3, length, local), BF16),
            jax.ShapeDtypeStruct((5, length, local), F32),
        ),
        in_specs=[pl.BlockSpec(memory_space=pltpu.SMEM)]
        + [whole] * len(pieces)
        + [pl.BlockSpec(memory_space=pltpu.HBM), whole, whole],
        out_specs=(whole, whole, whole),
        scratch_shapes=[
            pltpu.VMEM((length, width), BF16),
            pltpu.VMEM((length + 16, local), F32),
            pltpu.VMEM(w_in.shape, w_in.dtype),
            pltpu.SemaphoreType.DMA((3, 1)),
        ],
        compiler_params=pltpu.CompilerParams(vmem_limit_bytes=24 * 2**20),
        cost_estimate=pl.CostEstimate(
            flops=6 * length * local * width, transcendentals=0, bytes_accessed=6 * local * width
        ),
        name="mix",
    )(order, *pieces, w_in, feat, inner)


def after(value, *events):
    return lax.optimization_barrier((value,) + events)[0]


def terms_kernel(summed, qkv, saved, inner, pool, out, pad, stack, sums, *, scale):
    taps_kernel(summed, qkv, saved, inner, pool, sums, pad, stack)
    out[...] = (sums[...] * scale).astype(BF16)


def filter_terms(summed, qkv, saved, inner, groups, scale):
    length, local = qkv.shape[1:]
    member = jnp.arange(local)[:, None] // (local // groups) == jnp.arange(groups)[None, :]
    return pl.pallas_call(
        functools.partial(terms_kernel, scale=scale),
        out_shape=jax.ShapeDtypeStruct((32, groups), BF16),
        scratch_shapes=[
            pltpu.VMEM((length + 16, local), F32),
            pltpu.VMEM((32, local), F32),
            pltpu.VMEM((32, groups), F32),
        ],
        cost_estimate=FREE,
        name="filter_terms",
    )(summed, qkv, saved, inner, member.astype(F32))


def hop_all(piece, size):
    send = functools.partial(exchange, axis="fsdp", size=size)
    have = {0: piece}
    for z in (4, 8, 12):
        have[z] = send(piece, bits=z)
    for z in (0, 4, 8, 12):
        have[z + 2] = send(have[z], bits=2)
    for near in (0, 4, 2, 6, 8, 10, 12, 14):
        have[near + 1] = send(have[near], bits=1)
    return have


def both_ways(value, bits, size):
    half = value.astype(BF16)
    return half.astype(F32) + exchange(half, "fsdp", size, bits).astype(F32)


def tuned_device(ids, embed, gain, w_in, feat_filter, inner_filter, w_out, cotangent, right_prev):
    size = lax.axis_size("fsdp")
    count = lax.axis_size("dp")
    tokens = ids[0]
    length = tokens.shape[0]
    vocab, width = embed.shape
    local = w_in.shape[1]
    rank = right_prev.shape[1]
    index = lax.axis_index("fsdp").astype(jnp.int32)
    order = jnp.bitwise_xor(index, jnp.array(RELATIVE, jnp.int32))
    flag = lax.axis_index("dp").astype(jnp.int32)[None]
    send = functools.partial(exchange, axis="fsdp", size=size)
    feat = spread(feat_filter, local)
    inner = spread(inner_filter, local)

    onehot = (tokens[:, None] == jnp.arange(vocab, dtype=jnp.int32)[None, :]).astype(BF16)
    x_cols = jnp.dot(onehot, embed, preferred_element_type=F32).astype(BF16)
    x_sent = jnp.concatenate([x_cols, jnp.broadcast_to(gain[None, :], (EXTRA, width))], axis=0)
    have = hop_all(x_sent, size)
    w_in = pltpu.with_memory_space_constraint(w_in, pltpu.HBM)
    w_out = pltpu.with_memory_space_constraint(w_out, pltpu.HBM)

    cot_cols = cotangent[0]
    turns = [c + x + f + n for c in (1, 0) for x in (2, 0) for n in (4, 0) for f in (8, 0)]
    targets = jnp.bitwise_xor(index, jnp.array(turns, jnp.int32))
    away, keep = grad_parts(targets, w_out, cot_cols, size)
    keep = keep.astype(F32) + send(away, bits=1).astype(F32)
    away, keep = keep[:4].astype(BF16), keep[4:]
    side = jnp.dot(cot_cols, right_prev, preferred_element_type=F32)
    side = both_ways(side, 1, size)
    ready = after(order, side, away, keep)
    y, qkv, saved = mix_whole(ready, [have[r] for r in RELATIVE], w_in, feat, inner)

    keep = keep + send(away, bits=2).astype(F32)
    keep = keep[2:] + send(keep[:2].astype(BF16), bits=4).astype(F32)
    y_grad = (keep[1:] + send(keep[:1].astype(BF16), bits=8).astype(F32))[0]
    for bits in (2, 4, 8):
        side = both_ways(side, bits, size)
    side_other = exchange(side, "dp", count, 1)

    y_other = exchange(y, "dp", count, 1)
    got = hop_all(jnp.concatenate([y, y_other], axis=0), size)
    cot_other = exchange(after(cot_cols, got[4]), "dp", count, 1)
    groups = feat_filter.shape[1]
    scale = 1.0 / math.sqrt(count * length)
    terms = filter_terms(after(y_grad, got[12]), qkv, saved, inner, groups, scale)
    terms_other = exchange(terms, "dp", count, 1)
    filter_grad = terms.astype(F32) + terms_other.astype(F32)
    filter_grad = jnp.swapaxes(filter_grad.reshape(4, 8, groups), 1, 2)[:, :, : inner.shape[0]]
    got[15] = send(after(got[14], terms), bits=1)
    pieces = [got[r] for r in RELATIVE]
    block_out, basis, right_raw, sums = finish(
        flag, order, pieces, side, side_other, cot_cols, cot_other, x_sent, w_out
    )
    column_sums = plane_sum(sums, size)
    right_factor = right_raw * lax.rsqrt(column_sums / (size * width) + 1e-06)
    return (block_out[None], filter_grad, basis, right_factor)


def per_device(ids, embed, gain, w_in, feat_filter, inner_filter, w_out, cotangent, right_prev):
    sizes = (lax.axis_size("dp"), lax.axis_size("fsdp"))
    shapes = (ids.shape[1], w_in.shape[1], right_prev.shape[1])
    body = tuned_device if sizes == (2, 16) and shapes == (192, 256, 256) else general_device
    return body(ids, embed, gain, w_in, feat_filter, inner_filter, w_out, cotangent, right_prev)


def solution(mesh):
    placed = (
        P("dp", None),
        P(None, "fsdp"),
        P("fsdp"),
        P(None, "fsdp", None),
        P(None, "fsdp", None),
        P("fsdp", None),
        P(None, "fsdp"),
        P("dp", None, "fsdp"),
        P("fsdp", None),
    )
    return jax.shard_map(
        per_device,
        mesh=mesh,
        in_specs=placed,
        out_specs=(P("dp", None, "fsdp"), P(None, "fsdp", None), P("fsdp", None), P("fsdp", None)),
        check_vma=False,
    )
```
